32 devices in a mesh: coord: 8 (over z, y), cohort: 4 (over x, core).
Axes of the slice: x: 2, y: 2, z: 4, core: 2. Of those that a mesh axis runs over, the one named last changes fastest.
Arguments:
- shapes: bfloat16 [4, 1024, 32768], P('cohort', None, 'coord'), may hold values from -6 to 6
- sketch_signs: int32 [4, 1024, 128], P('cohort'), may hold values from -1 to 1
- merge_sketch: float32 [2, 2, 128, 128], replicated, may hold values from -1.5 to 1.5
Outputs:
- basis: float32 [4, 32768, 128], P('cohort', 'coord')
- scores: float32 [4, 1024, 128], P('cohort', 'coord')
The draws below stay inside these ranges and needn't reach their ends.
All inputs are finite; a program needn't handle non-finite values.
Results may differ from the reference program's by a relative error of at most 0.0086.
Values sent between devices are 32-bit elements; how exact they have to be, the bound alone decides.
A program may use at most 64 MiB of HBM per device.

```python
import math
import jax
import jax.numpy as jnp
from jax import lax

K = 128
SUBJ = 1024
LEVELS = 2
P_SIZE = 32768
COHORTS = 4


def draw_shapes(key, part):
    mode_key = jax.random.fold_in(key, 11)
    own_key = jax.random.fold_in(key, 12)
    coef_key = jax.random.fold_in(key, 13)
    noise_key = jax.random.fold_in(key, 14)
    modes = jax.random.normal(mode_key, (K, P_SIZE), jnp.float32)
    spread = 0.3 * jnp.power(0.97, jnp.arange(K, dtype=jnp.float32))
    coefs = jax.random.normal(coef_key, (COHORTS, SUBJ, K), jnp.float32) * spread
    own = jax.random.normal(own_key, (COHORTS, K, P_SIZE), jnp.float32)
    cohort_modes = modes[None] + 0.2 * own
    signal = jnp.einsum('csk,ckp->csp', coefs, cohort_modes)
    noise = 0.3 * jax.random.normal(noise_key, (COHORTS, SUBJ, P_SIZE), jnp.float32)
    values = signal + noise
    return jnp.clip(values, -6.0, 6.0).astype(jnp.bfloat16)


def draw_merge_sketch(key, part):
    mix_key = jax.random.fold_in(key, 21)
    noise = jnp.clip(jax.random.normal(mix_key, (LEVELS, 2, K, K), jnp.float32), -6.0, 6.0)
    noise = noise * (0.2 * K ** (-0.5))
    ident = jnp.eye(K, dtype=jnp.float32)
    lower_map = ident[None] + noise[:, 0]
    upper_map = noise[:, 1]
    return jnp.stack([lower_map, upper_map], axis=1)


def set_ends(entries, key, smallest, top_value):
    longest = entries.shape.index(max(entries.shape))
    spots = []
    for shift in (0, 1):
        where = [jax.random.randint(jax.random.fold_in(key, axis), (), 0, length) for axis, length in enumerate(entries.shape)]
        where[longest] = (where[longest] + shift) % entries.shape[longest]
        spots.append(tuple(where))
    return entries.at[spots[0]].set(smallest).at[spots[1]].set(top_value)


def setup_inputs(seed: int = 0) -> dict:
    splits = jax.random.split(jax.random.key(seed), 4)
    return {
        "shapes": draw_shapes(jax.random.fold_in(splits[3], 71), 0),
        "sketch_signs": set_ends(jax.random.randint(splits[1], (COHORTS, SUBJ, K), -1, 2), jax.random.fold_in(splits[1], 1), -1, 1).astype(jnp.int32),
        "merge_sketch": draw_merge_sketch(jax.random.fold_in(splits[3], 71), 0),
    }


def lower_inverse_t(gram):
    factor = jnp.linalg.cholesky(gram)
    ident = jnp.eye(gram.shape[0], dtype=gram.dtype)
    inverse = jax.scipy.linalg.solve_triangular(factor, ident, lower=True)
    return inverse.T

def orthonormal(mixed):
    gram = jnp.dot(mixed.T, mixed, precision=lax.Precision.HIGHEST)
    return jnp.dot(mixed, lower_inverse_t(gram), precision=lax.Precision.HIGHEST)

def reference(shapes, sketch_signs, merge_sketch):
    count = shapes.shape[0]
    centered_all = []
    bases = []
    for cohort in range(count):
        data = shapes[cohort].astype(jnp.float32)
        centered = (data - lax.optimization_barrier(jnp.mean(data, axis=0, keepdims=True))).astype(jnp.bfloat16)
        centered_all.append(centered)
        signs = sketch_signs[cohort].astype(jnp.bfloat16)
        sketch = jnp.dot(centered.T.astype(jnp.float32), signs.astype(jnp.float32), preferred_element_type=jnp.float32)
        bases.append(orthonormal(sketch))
    for level in range(LEVELS):
        merged = []
        for cohort in range(count):
            lower = cohort & ~(1 << level)
            upper = lower | 1 << level
            mixed = jnp.dot(bases[lower], merge_sketch[level, 0], precision=lax.Precision.HIGHEST)
            mixed = mixed + jnp.dot(bases[upper], merge_sketch[level, 1], precision=lax.Precision.HIGHEST)
            merged.append(orthonormal(mixed))
        bases = merged
    factor = 4.0 * math.sqrt(K / P_SIZE)
    basis_out = jnp.stack([b * math.sqrt(P_SIZE) for b in bases])
    score_out = jnp.stack([jnp.dot(centered_all[c].astype(jnp.float32), bases[c].astype(jnp.bfloat16).astype(jnp.float32), preferred_element_type=jnp.float32) * factor for c in range(count)])
    return (basis_out, score_out)
```

```python
import functools
import math

import jax
import jax.numpy as jnp
from jax import lax
from jax.experimental import pallas as pl
from jax.experimental.pallas import tpu as pltpu
from jax.sharding import PartitionSpec as P

HIGHEST = lax.Precision.HIGHEST
MESH = pl.DeviceIdType.MESH
F32 = jnp.float32
BF16 = jnp.bfloat16


def dot(a, b):
    return jnp.dot(a, b, preferred_element_type=F32)


def dot_high(a, b, dims):
    return lax.dot_general(a, b, (dims, ((), ())), precision=HIGHEST, preferred_element_type=F32)


def split(x):
    high = x.astype(BF16)
    return high, (x - high.astype(F32)).astype(BF16)


def cross_product(a, b):
    dims = (((0,), (0,)), ((), ()))
    a_high, a_mid = split(a)
    b_high, b_mid = split(b)
    wide = lax.dot_general(
        a_high, jnp.concatenate([b_high, b_mid], axis=1), dims, preferred_element_type=F32
    )
    width = b.shape[1]
    return (
        wide[:, :width]
        + wide[:, width:]
        + lax.dot_general(a_mid, b_high, dims, preferred_element_type=F32)
    )


def stack_map(stacked, which, value):
    high, mid = split(value)
    width = value.shape[0]
    base = 3 * width * which
    stacked[base : base + width, :] = high
    stacked[base + width : base + 2 * width, :] = high
    stacked[base + 2 * width : base + 3 * width, :] = mid


def mix_rows(low, up, stacked):
    low_high, low_mid = split(low)
    up_high, up_mid = split(up)
    rows = jnp.concatenate([low_high, low_mid, low_high, up_high, up_mid, up_high], axis=1)
    return dot(rows, stacked[...])


def inverse_of(gram, x_ref):
    size = gram.shape[1]
    step = 8
    tiles = size // step
    lane = lax.broadcasted_iota(jnp.int32, (step, size), 1)
    sub = lax.broadcasted_iota(jnp.int32, (step, size), 0)

    def full(x):
        return jnp.broadcast_to(x, (step, size))

    def total(terms):
        while len(terms) > 1:
            terms = [terms[i] + terms[i + 1] for i in range(0, len(terms), 2)]
        return terms[0]

    left = gram.reshape(tiles, step, size)
    right = jnp.stack([(lane == sub + t * step).astype(F32) for t in range(tiles)])
    for t in range(tiles):
        at = t * step
        head, head_x = left[0], right[0]
        cols = [full(head[:, at + k : at + k + 1]) for k in range(step)]
        e = [[full(cols[k][i : i + 1, :]) for k in range(i + 1)] for i in range(step)]
        rows = [full(head[i : i + 1, :]) for i in range(step)]
        rows_x = [full(head_x[i : i + 1, :]) for i in range(step)]
        f = {}
        inv = []
        for s in range(step):
            inv.append(1.0 / e[s][s])
            for i in range(s + 1, step):
                f[i, s] = e[i][s] * inv[s]
                for k in range(s + 1, i + 1):
                    e[i][k] = e[i][k] - f[i, s] * e[k][s]
            for i in range(s + 1, step):
                rows[i] = rows[i] - f[i, s] * rows[s]
                rows_x[i] = rows_x[i] - f[i, s] * rows_x[s]
        out = rows_x[0] * lax.rsqrt(e[0][0])
        for s in range(1, step):
            out = jnp.where(sub == s, rows_x[s] * lax.rsqrt(e[s][s]), out)
        x_ref[at : at + step, :] = out
        if t + 1 == tiles:
            break
        rows = [rows[s] * inv[s] for s in range(step)]
        rows_x = [rows_x[s] * inv[s] for s in range(step)]
        for s in range(step - 2, -1, -1):
            for i in range(s + 1, step):
                rows[s] = rows[s] - f[i, s] * rows[i]
                rows_x[s] = rows_x[s] - f[i, s] * rows_x[i]
        left, right = left[1:], right[1:]
        c = [jnp.broadcast_to(left[:, :, at + s : at + s + 1], left.shape) for s in range(step)]
        left = left - total([c[s] * rows[s][None] for s in range(step)])
        right = right - total([c[s] * rows_x[s][None] for s in range(step)])


def remote(src, dst, send, got, device):
    return pltpu.make_async_remote_copy(
        src_ref=src, dst_ref=dst, send_sem=send, recv_sem=got, device_id=device, device_id_type=MESH
    )


def scatter(part, recv, group, send, got):
    me, size, ident = group
    copies = []
    for d in range(1, size):
        peer = lax.rem(me + d, size)
        copies.append(remote(part.at[peer], recv.at[d], send.at[d], got.at[d], ident(peer)))
    return copies


def start(copies):
    for copy in copies:
        copy.start()


def summed(part, recv, group, copies):
    me, size, ident = group
    total = part[me]
    for d in range(1, size):
        copies[d - 1].wait_recv()
        total = total + recv[d]
    return total


def spread(out, group, send, got):
    me, size, ident = group
    return [
        remote(out.at[me], out.at[me], send.at[d], got.at[d], ident(lax.rem(me + d, size)))
        for d in range(1, size)
    ]


def received(copies):
    for copy in copies:
        copy.wait_recv()


def sent(copies):
    for copy in copies:
        copy.wait_send()


def whole_kernel(
    n, tile, shapes_ref, signs_ref, merge_ref, basis_ref, scores_ref,
    held, signs, merge, turned, given, pairs, mixed, stacked, maps, outer, x_ref, narrow,
    wide, products, gram_part, gram_recv, gram, low_part, low_recv, low_gram,
    up_part, up_recv, up_gram, up_other, score_part, score_recv,
    loaded, small, give_send, give_got, gram_send, gram_got, gram_send2, gram_got2,
    low_send, low_got, low_send2, low_got2, up_send, up_got, up_send2, up_got2,
    cross_send, cross_got, basis_send, basis_got, score_send, score_got, map_send, map_got,
):
    coord = lax.axis_index("coord")
    cohort = lax.axis_index("cohort")
    side = lax.rem(cohort, 2)
    upper = lax.rem(cohort // 2, 2)
    base = cohort - side
    partner = {"cohort": cohort + 1 - 2 * side}
    across = {"cohort": cohort + 2 - 4 * upper}
    line = (coord, n, lambda r: {"coord": r})
    pair = (
        coord * 2 + side, 2 * n, lambda r: {"coord": r // 2, "cohort": base + lax.rem(r, 2)}
    )
    chunks = held.shape[0] // 2
    half = chunks * tile
    width = turned.shape[0]

    def rows_of(c):
        return pl.ds(pl.multiple_of(c * tile, tile), tile)

    small_copies = [
        pltpu.make_async_copy(signs_ref, signs, small.at[0]),
        pltpu.make_async_copy(merge_ref, merge, small.at[1]),
    ]
    start(small_copies)

    def load(h, c):
        at = pl.multiple_of((h * chunks + c) * tile, tile)
        return pltpu.make_async_copy(
            shapes_ref.at[:, pl.ds(at, tile)], held.at[h * chunks + c], loaded.at[h, c]
        )

    for h in (1 - side, side):
        for c in range(chunks):
            load(h, c).start()

    barrier = pltpu.get_barrier_semaphore()
    me, size, ident = pair
    for d in range(1, size):
        pl.semaphore_signal(
            barrier, inc=1, device_id=ident(lax.rem(me + d, size)), device_id_type=MESH
        )
    pl.semaphore_signal(barrier, inc=1, device_id=across, device_id_type=MESH)
    for copy in small_copies:
        copy.wait()
    turned[...] = signs[...].astype(F32).T.astype(BF16)
    for l in range(2):
        outer[l] = dot_high(merge[l, 0], merge[l, 0], ((0,), (0,))) + dot_high(
            merge[l, 1], merge[l, 1], ((0,), (0,))
        )
    wide[...] = jnp.zeros_like(wide)
    pl.semaphore_wait(barrier, size)

    def give(c):
        return remote(
            given.at[rows_of(c)], pairs.at[side, rows_of(c)], give_send.at[c], give_got.at[c], partner
        )

    def sketch(h, c):
        load(h, c).wait()
        block = held.at[h * chunks + c]
        mean = jnp.sum(block[...].astype(F32), axis=0, keepdims=True) * (1.0 / block.shape[0])
        block[...] = (block[...].astype(F32) - mean).astype(BF16)
        flat = dot(turned[...], block[...])
        rows = flat.T
        high, mid = split(rows)
        wide[...] += dot(flat.astype(BF16), jnp.concatenate([high, mid], axis=1))
        return rows

    def first(c, carry):
        given[rows_of(c)] = sketch(1 - side, c)
        give(c).start()
        return carry

    def second(c, carry):
        pairs[side, rows_of(c)] = sketch(side, c)
        return carry

    lax.fori_loop(0, chunks, first, 0)
    lax.fori_loop(0, chunks, second, 0)
    turn = wide[:, width:]
    own = wide[:, :width] + turn + turn.T
    gram_part[...] = own.reshape(gram_part.shape)
    copies = scatter(gram_part, gram_recv, line, gram_send, gram_got)
    start(copies)

    products[...] = jnp.zeros_like(products)

    def cross(c, carry):
        give(c).wait_recv()
        products[...] += cross_product(pairs[0, rows_of(c)], pairs[1, rows_of(c)])
        return carry

    lax.fori_loop(0, chunks, cross, 0)
    low_part[...] = products[...].reshape(low_part.shape)
    gram[coord] = summed(gram_part, gram_recv, line, copies)
    gathered = spread(gram, line, gram_send2, gram_got2)
    start(gathered)
    low_copies = scatter(low_part, low_recv, pair, low_send, low_got)
    start(low_copies)
    received(gathered)

    inverse_of(gram[...].reshape(width, width), x_ref)
    maps[0, side] = dot_high(x_ref[...], merge[0, side], ((0,), (0,)))
    map_swap = remote(maps.at[0, side], maps.at[0, side], map_send.at[0], map_got.at[0], partner)
    map_swap.start()
    low_gram[pair[0]] = summed(low_part, low_recv, pair, low_copies)
    low_gathered = spread(low_gram, pair, low_send2, low_got2)
    start(low_gathered)
    map_swap.wait_recv()
    for i in range(2):
        stack_map(stacked, i, maps[0, i])

    def ship(c):
        return remote(
            mixed.at[upper, rows_of(c)], mixed.at[upper, rows_of(c)],
            cross_send.at[c], cross_got.at[c], across,
        )

    def turn_of(which, i):
        return lax.rem(i + which * (chunks // 2), chunks)

    def blend(i, carry):
        c = turn_of(upper, i)
        mixed[upper, rows_of(c)] = mix_rows(pairs[0, rows_of(c)], pairs[1, rows_of(c)], stacked)
        ship(c).start()
        return carry

    lax.fori_loop(0, chunks, blend, 0)
    received(low_gathered)
    inner = dot_high(
        maps[0, 0],
        dot_high(low_gram[...].reshape(width, width), maps[0, 1], ((1,), (0,))),
        ((0,), (0,)),
    )
    inverse_of(outer[0] + inner + inner.T, x_ref)
    maps[1, upper] = dot_high(x_ref[...], merge[1, upper], ((0,), (0,)))
    across_swap = remote(maps.at[1, upper], maps.at[1, upper], map_send.at[1], map_got.at[1], across)
    across_swap.start()

    products[...] = jnp.zeros_like(products)

    def meet(i, carry):
        c = turn_of(1 - upper, i)
        ship(c).wait_recv()
        products[...] += cross_product(mixed[0, rows_of(c)], mixed[1, rows_of(c)])
        return carry

    lax.fori_loop(0, chunks // 2, meet, 0)
    up_part[...] = products[...].reshape(up_part.shape)
    up_copies = scatter(up_part, up_recv, pair, up_send, up_got)
    start(up_copies)
    up_other[upper] = summed(up_part, up_recv, pair, up_copies)
    up_swap = remote(up_other.at[upper], up_other.at[upper], map_send.at[2], map_got.at[2], across)
    up_swap.start()
    up_swap.wait_recv()
    up_gram[pair[0]] = up_other[0] + up_other[1]
    up_gathered = spread(up_gram, pair, up_send2, up_got2)
    start(up_gathered)
    across_swap.wait_recv()
    received(up_gathered)
    inner = dot_high(
        maps[1, 0],
        dot_high(up_gram[...].reshape(width, width), maps[1, 1], ((1,), (0,))),
        ((0,), (0,)),
    )
    inverse_of(outer[1] + inner + inner.T, x_ref)
    for i in range(2):
        stack_map(stacked, i, dot_high(maps[1, i], x_ref[...], ((1,), (1,))))

    def hand(c):
        return remote(
            basis_ref.at[side, rows_of(c)], basis_ref.at[side, rows_of(c)],
            basis_send.at[c], basis_got.at[c], partner,
        )

    def finish(c):
        rows = mix_rows(mixed[0, rows_of(c)], mixed[1, rows_of(c)], stacked)
        basis_ref[side, rows_of(c)] = rows
        narrow[side * chunks + c] = rows.astype(BF16)
        hand(c).start()


    def arriving(i, carry):
        c = turn_of(1 - upper, i)
        ship(c).wait_recv()
        finish(c)
        return carry

    def local(i, carry):
        finish(turn_of(1 - upper, i))
        return carry

    lax.fori_loop(0, chunks // 2, local, 0)
    lax.fori_loop(chunks // 2, chunks, arriving, 0)

    block = score_part.shape[1]
    order = [lax.rem(coord + d, n) for d in list(range(1, n)) + [0]]

    def taken(peer, h):
        rows = pl.ds(pl.multiple_of(peer * block, block), block)
        total = dot(held[h * chunks, rows], narrow[h * chunks])
        for c in range(1, chunks):
            total = total + dot(held[h * chunks + c, rows], narrow[h * chunks + c])
        return total

    for peer in order:
        score_part[peer] = taken(peer, side)
    for c in range(chunks):
        hand(c).wait_recv()
        narrow[(1 - side) * chunks + c] = basis_ref[1 - side, rows_of(c)].astype(BF16)
    score_copies = scatter(score_part, score_recv, line, score_send, score_got)
    for d, peer in zip(list(range(1, n)) + [0], order):
        score_part[peer] = score_part[peer] + taken(peer, 1 - side)
        if d:
            score_copies[d - 1].start()
    scores_ref[...] = summed(score_part, score_recv, line, score_copies)

    sent(copies + gathered + low_copies + low_gathered + up_copies + up_gathered + score_copies)
    sent([map_swap, across_swap, up_swap])
    for c in range(chunks):
        give(c).wait_send()
        ship(c).wait_send()
        hand(c).wait_send()


def on_device(shapes, sketch_signs, merge_sketch):
    n = lax.axis_size("coord")
    _, subjects, coords = shapes.shape
    width = sketch_signs.shape[2]
    half = coords // 2
    tile = math.gcd(half // 2, 512)
    chunks = half // tile
    rows = subjects // n
    line = (n, width // n, width)
    pair = (2 * n, width // (2 * n), width)
    vmem, dma = pltpu.VMEM, pltpu.SemaphoreType.DMA
    basis, scores = pl.pallas_call(
        functools.partial(whole_kernel, n, tile),
        out_shape=(
            jax.ShapeDtypeStruct((2, half, width), F32),
            jax.ShapeDtypeStruct((rows, width), F32),
        ),
        in_specs=[pl.BlockSpec(memory_space=pl.ANY)] * 3,
        out_specs=(pl.BlockSpec(memory_space=vmem), pl.BlockSpec(memory_space=vmem)),
        scratch_shapes=[
            vmem((2 * chunks, subjects, tile), BF16),
            vmem((subjects, width), jnp.int32),
            vmem(merge_sketch.shape, F32),
            vmem((width, subjects), BF16),
            vmem((half, width), F32),
            vmem((2, half, width), F32),
            vmem((2, half, width), F32),
            vmem((6 * width, width), BF16),
            vmem((2, 2, width, width), F32),
            vmem((2, width, width), F32),
            vmem((width, width), F32),
            vmem((2 * chunks, tile, width), BF16),
            vmem((width, 2 * width), F32),
            vmem((width, width), F32),
            vmem(line, F32),
            vmem(line, F32),
            vmem(line, F32),
            vmem(pair, F32),
            vmem(pair, F32),
            vmem(pair, F32),
            vmem(pair, F32),
            vmem(pair, F32),
            vmem(pair, F32),
            vmem((2,) + pair[1:], F32),
            vmem((n, rows, width), F32),
            vmem((n, rows, width), F32),
            dma((2, chunks)),
            dma((2,)),
            dma((chunks,)),
            dma((chunks,)),
        ]
        + [dma((n,))] * 4
        + [dma((2 * n,))] * 8
        + [dma((chunks,))] * 4
        + [dma((n,))] * 2
        + [dma((3,))] * 2,
        compiler_params=pltpu.CompilerParams(
            collective_id=0, has_side_effects=True, vmem_limit_bytes=48 * 1024 * 1024
        ),
        name="shape_pca",
    )(shapes[0], sketch_signs[0], merge_sketch)
    total_coords = coords * n
    basis = basis.reshape(coords, width) * math.sqrt(total_coords)
    scores = scores * (4.0 * math.sqrt(width / total_coords))
    return basis[None], scores[None]


def solution(mesh):
    placed = (P("cohort", None, "coord"), P("cohort", None, None), P())
    return jax.shard_map(
        on_device,
        mesh=mesh,
        in_specs=placed,
        out_specs=(P("cohort", "coord", None), P("cohort", "coord", None)),
        check_vma=False,
    )
```

```python
import functools
import math

import jax
import jax.numpy as jnp
from jax import lax
from jax.experimental import pallas as pl
from jax.experimental.pallas import tpu as pltpu
from jax.sharding import PartitionSpec as P

HIGHEST = lax.Precision.HIGHEST
MESH = pl.DeviceIdType.MESH
F32 = jnp.float32
BF16 = jnp.bfloat16


def dot(a, b):
    return jnp.dot(a, b, preferred_element_type=F32)


def dot_high(a, b, dims):
    return lax.dot_general(a, b, (dims, ((), ())), precision=HIGHEST, preferred_element_type=F32)


def split(x):
    high = x.astype(BF16)
    return high, (x - high.astype(F32)).astype(BF16)


def cross_product(a, b):
    dims = (((0,), (0,)), ((), ()))
    a_high, a_mid = split(a)
    b_high, b_mid = split(b)
    wide = lax.dot_general(
        a_high, jnp.concatenate([b_high, b_mid], axis=1), dims, preferred_element_type=F32
    )
    width = b.shape[1]
    return (
        wide[:, :width]
        + wide[:, width:]
        + lax.dot_general(a_mid, b_high, dims, preferred_element_type=F32)
    )


def stack_map(stacked, which, value):
    high, mid = split(value)
    width = value.shape[0]
    base = 3 * width * which
    stacked[base : base + width, :] = high
    stacked[base + width : base + 2 * width, :] = high
    stacked[base + 2 * width : base + 3 * width, :] = mid


def mix_rows(low, up, stacked):
    low_high, low_mid = split(low)
    up_high, up_mid = split(up)
    rows = jnp.concatenate([low_high, low_mid, low_high, up_high, up_mid, up_high], axis=1)
    return dot(rows, stacked[...])


def inverse_of(gram, x_ref):
    size = gram.shape[1]
    step = 8
    tiles = size // step
    lane = lax.broadcasted_iota(jnp.int32, (step, size), 1)
    sub = lax.broadcasted_iota(jnp.int32, (step, size), 0)

    def full(x):
        return jnp.broadcast_to(x, (step, size))

    def total(terms):
        while len(terms) > 1:
            terms = [terms[i] + terms[i + 1] for i in range(0, len(terms), 2)]
        return terms[0]

    left = gram.reshape(tiles, step, size)
    right = jnp.stack([(lane == sub + t * step).astype(F32) for t in range(tiles)])
    for t in range(tiles):
        at = t * step
        head, head_x = left[0], right[0]
        cols = [full(head[:, at + k : at + k + 1]) for k in range(step)]
        e = [[full(cols[k][i : i + 1, :]) for k in range(i + 1)] for i in range(step)]
        rows = [full(head[i : i + 1, :]) for i in range(step)]
        rows_x = [full(head_x[i : i + 1, :]) for i in range(step)]
        f = {}
        inv = []
        for s in range(step):
            inv.append(1.0 / e[s][s])
            for i in range(s + 1, step):
                f[i, s] = e[i][s] * inv[s]
                for k in range(s + 1, i + 1):
                    e[i][k] = e[i][k] - f[i, s] * e[k][s]
            for i in range(s + 1, step):
                rows[i] = rows[i] - f[i, s] * rows[s]
                rows_x[i] = rows_x[i] - f[i, s] * rows_x[s]
        out = rows_x[0] * lax.rsqrt(e[0][0])
        for s in range(1, step):
            out = jnp.where(sub == s, rows_x[s] * lax.rsqrt(e[s][s]), out)
        x_ref[at : at + step, :] = out
        if t + 1 == tiles:
            break
        rows = [rows[s] * inv[s] for s in range(step)]
        rows_x = [rows_x[s] * inv[s] for s in range(step)]
        for s in range(step - 2, -1, -1):
            for i in range(s + 1, step):
                rows[s] = rows[s] - f[i, s] * rows[i]
                rows_x[s] = rows_x[s] - f[i, s] * rows_x[i]
        left, right = left[1:], right[1:]
        c = [jnp.broadcast_to(left[:, :, at + s : at + s + 1], left.shape) for s in range(step)]
        left = left - total([c[s] * rows[s][None] for s in range(step)])
        right = right - total([c[s] * rows_x[s][None] for s in range(step)])


def remote(src, dst, send, got, device):
    return pltpu.make_async_remote_copy(
        src_ref=src, dst_ref=dst, send_sem=send, recv_sem=got, device_id=device, device_id_type=MESH
    )


def scatter(part, recv, group, send, got):
    me, size, ident = group
    copies = []
    for d in range(1, size):
        peer = lax.rem(me + d, size)
        copies.append(remote(part.at[peer], recv.at[d], send.at[d], got.at[d], ident(peer)))
    return copies


def start(copies):
    for copy in copies:
        copy.start()


def summed(part, recv, group, copies):
    me, size, ident = group
    total = part[me]
    for d in range(1, size):
        copies[d - 1].wait_recv()
        total = total + recv[d]
    return total


def spread(out, group, send, got):
    me, size, ident = group
    return [
        remote(out.at[me], out.at[me], send.at[d], got.at[d], ident(lax.rem(me + d, size)))
        for d in range(1, size)
    ]


def received(copies):
    for copy in copies:
        copy.wait_recv()


def sent(copies):
    for copy in copies:
        copy.wait_send()


def whole_kernel(
    n, tile, shapes_ref, signs_ref, merge_ref, basis_ref, scores_ref,
    held, signs, merge, turned, given, pairs, far, mixed, stacks, low_maps, up_maps, outer, x_ref,
    wide, products, projected, gram_part, gram_recv, gram, low_part, low_recv, low_gram,
    up_part, up_recv, up_gram, up_other, score_part, score_recv,
    loaded, small, give_send, give_got, far_send, far_got, core_send, core_got,
    cross_send, cross_got, gram_send, gram_got, gram_send2, gram_got2, score_send, score_got,
    low_send, low_got, low_send2, low_got2, up_send, up_got, up_send2, up_got2, map_send, map_got,
):
    coord = lax.axis_index("coord")
    cohort = lax.axis_index("cohort")
    side = lax.rem(cohort, 2)
    upper = lax.rem(cohort // 2, 2)
    base = cohort - side
    partner = {"cohort": cohort + 1 - 2 * side}
    across = {"cohort": cohort + 2 - 4 * upper}
    corner = {"cohort": cohort + 2 - 4 * upper + 1 - 2 * side}
    line = (coord, n, lambda r: {"coord": r})
    pair = (
        coord * 2 + side, 2 * n, lambda r: {"coord": r // 2, "cohort": base + lax.rem(r, 2)}
    )
    chunks = held.shape[0] // 2
    early = chunks // 2
    width = turned.shape[0]

    def rows_of(c):
        return pl.ds(pl.multiple_of(c * tile, tile), tile)

    def turn_of(which, i):
        return lax.rem(i + which * early, chunks)

    small_copies = [
        pltpu.make_async_copy(signs_ref, signs, small.at[0]),
        pltpu.make_async_copy(merge_ref, merge, small.at[1]),
    ]
    start(small_copies)

    def load(h, c):
        at = pl.multiple_of((h * chunks + c) * tile, tile)
        return pltpu.make_async_copy(
            shapes_ref.at[:, pl.ds(at, tile)], held.at[h * chunks + c], loaded.at[h, c]
        )

    for i in range(chunks):
        load(1 - side, turn_of(upper, i)).start()
        load(side, turn_of(upper, i)).start()

    barrier = pltpu.get_barrier_semaphore()
    me, size, ident = pair
    for d in range(1, size):
        pl.semaphore_signal(
            barrier, inc=1, device_id=ident(lax.rem(me + d, size)), device_id_type=MESH
        )
    pl.semaphore_signal(barrier, inc=1, device_id=across, device_id_type=MESH)
    pl.semaphore_signal(barrier, inc=1, device_id=corner, device_id_type=MESH)
    wide[...] = jnp.zeros_like(wide)
    products[...] = jnp.zeros_like(products)
    small_copies[0].wait()
    turned[...] = signs[...].astype(F32).T.astype(BF16)
    pl.semaphore_wait(barrier, size + 1)

    def give(c):
        return remote(
            given.at[rows_of(c)], pairs.at[side, rows_of(c)], give_send.at[c], give_got.at[c], partner
        )

    def far_given(i):
        return remote(
            given.at[rows_of(turn_of(upper, i))], far.at[side, i],
            far_send.at[0, i], far_got.at[0, i], corner,
        )

    def far_mine(i):
        return remote(
            pairs.at[side, rows_of(turn_of(upper, i))], far.at[side, i],
            far_send.at[1, i], far_got.at[1, i], across,
        )

    def sketch(h, c):
        load(h, c).wait()
        block = held.at[h * chunks + c]
        mean = jnp.sum(block[...].astype(F32), axis=0, keepdims=True) * (1.0 / block.shape[0])
        block[...] = (block[...].astype(F32) - mean).astype(BF16)
        flat = dot(turned[...], block[...])
        rows = flat.T
        high, mid = split(rows)
        wide[...] += dot(flat.astype(BF16), jnp.concatenate([high, mid], axis=1))
        return rows

    def first(i, carry):
        c = turn_of(upper, i)
        given[rows_of(c)] = sketch(1 - side, c)
        far_given(i).start()
        give(c).start()
        pairs[side, rows_of(c)] = sketch(side, c)
        far_mine(i).start()
        return carry

    def second(i, carry):
        c = turn_of(upper, i)
        given[rows_of(c)] = sketch(1 - side, c)
        give(c).start()
        pairs[side, rows_of(c)] = sketch(side, c)
        return carry

    lax.fori_loop(0, early, first, 0)
    lax.fori_loop(early, chunks, second, 0)
    turn = wide[:, width:]
    own = wide[:, :width] + turn + turn.T
    gram_part[...] = own.reshape(gram_part.shape)
    copies = scatter(gram_part, gram_recv, line, gram_send, gram_got)
    start(copies)

    def cross(c, carry):
        give(c).wait_recv()
        products[...] += cross_product(pairs[0, rows_of(c)], pairs[1, rows_of(c)])
        return carry

    lax.fori_loop(0, chunks, cross, 0)
    low_part[...] = products[...].reshape(low_part.shape)
    gram[coord] = summed(gram_part, gram_recv, line, copies)
    gathered = spread(gram, line, gram_send2, gram_got2)
    start(gathered)
    low_copies = scatter(low_part, low_recv, pair, low_send, low_got)
    start(low_copies)
    small_copies[1].wait()
    for l in range(2):
        outer[l] = dot_high(merge[l, 0], merge[l, 0], ((0,), (0,))) + dot_high(
            merge[l, 1], merge[l, 1], ((0,), (0,))
        )
    received(gathered)

    inverse_of(gram[...].reshape(width, width), x_ref)
    low_maps[upper, side] = dot_high(x_ref[...], merge[0, side], ((0,), (0,)))
    own_map = low_maps.at[upper, side]
    map_copies = [
        remote(own_map, own_map, map_send.at[i], map_got.at[i], device)
        for i, device in enumerate((partner, across, corner))
    ]
    start(map_copies)
    low_gram[pair[0]] = summed(low_part, low_recv, pair, low_copies)
    low_gathered = spread(low_gram, pair, low_send2, low_got2)
    start(low_gathered)
    map_copies[0].wait_recv()
    for i in range(2):
        stack_map(stacks.at[0], i, low_maps[upper, i])

    def ship(c):
        rows = mixed.at[upper, side, rows_of(c)]
        return remote(rows, rows, cross_send.at[c], cross_got.at[c], across)

    def share(which, c):
        far_side = lax.rem(which + upper, 2)
        rows = mixed.at[far_side, side, rows_of(c)]
        return remote(rows, rows, core_send.at[which, c], core_got.at[which, c], partner)

    def blend(i):
        c = turn_of(upper, i)
        mixed[upper, side, rows_of(c)] = mix_rows(
            pairs[0, rows_of(c)], pairs[1, rows_of(c)], stacks.at[0]
        )
        share(0, c).start()
        return c

    for i in range(early, chunks):
        c = blend(i)
        if i < chunks - 1:
            ship(c).start()
    late = turn_of(upper, chunks - 1)
    for i in range(early):
        blend(i)
    received(map_copies[1:])
    for i in range(2):
        stack_map(stacks.at[1], i, low_maps[1 - upper, i])

    products[...] = jnp.zeros_like(products)

    def meet(i, carry):
        c = turn_of(1 - upper, i)
        far_given(i).wait_recv()
        far_mine(i).wait_recv()
        mixed[1 - upper, side, rows_of(c)] = mix_rows(far[0, i], far[1, i], stacks.at[1])
        share(1, c).start()
        products[...] += cross_product(mixed[0, side, rows_of(c)], mixed[1, side, rows_of(c)])
        return carry

    lax.fori_loop(0, early, meet, 0)
    up_part[...] = products[...].reshape(up_part.shape)
    up_copies = scatter(up_part, up_recv, pair, up_send, up_got)
    start(up_copies)
    received(low_gathered)
    inner = dot_high(
        low_maps[upper, 0],
        dot_high(low_gram[...].reshape(width, width), low_maps[upper, 1], ((1,), (0,))),
        ((0,), (0,)),
    )
    inverse_of(outer[0] + inner + inner.T, x_ref)
    up_maps[upper] = dot_high(x_ref[...], merge[1, upper], ((0,), (0,)))
    up_other[upper] = summed(up_part, up_recv, pair, up_copies)
    up_swap = remote(up_other.at[upper], up_other.at[upper], map_send.at[3], map_got.at[3], across)
    up_swap.start()
    across_swap = remote(
        up_maps.at[upper], up_maps.at[upper], map_send.at[4], map_got.at[4], across
    )
    across_swap.start()
    ship(late).start()

    projected[...] = jnp.zeros_like(projected)

    def project(h, c):
        rows = jnp.concatenate(
            [mixed[0, h, rows_of(c)].astype(BF16), mixed[1, h, rows_of(c)].astype(BF16)], axis=1
        )
        projected[...] += dot(held[h * chunks + c], rows)

    def project_early(i, carry):
        c = turn_of(1 - upper, i)
        project(side, c)
        share(0, c).wait_recv()
        share(1, c).wait_recv()
        project(1 - side, c)
        return carry

    def project_late(i, carry):
        c = turn_of(1 - upper, i)
        ship(c).wait_recv()
        share(1, c).start()
        project(side, c)
        return carry

    def project_last(i, carry):
        c = turn_of(1 - upper, i)
        share(0, c).wait_recv()
        share(1, c).wait_recv()
        project(1 - side, c)
        return carry

    lax.fori_loop(0, 1, project_early, 0)
    up_swap.wait_recv()
    up_gram[pair[0]] = up_other[0] + up_other[1]
    up_gathered = spread(up_gram, pair, up_send2, up_got2)
    start(up_gathered)
    lax.fori_loop(1, early, project_early, 0)
    lax.fori_loop(early, chunks, project_late, 0)
    across_swap.wait_recv()
    received(up_gathered)
    inner = dot_high(
        up_maps[0],
        dot_high(up_gram[...].reshape(width, width), up_maps[1], ((1,), (0,))),
        ((0,), (0,)),
    )
    inverse_of(outer[1] + inner + inner.T, x_ref)
    for i in range(2):
        stack_map(stacks.at[0], i, dot_high(up_maps[i], x_ref[...], ((1,), (1,))))
    lax.fori_loop(early, chunks, project_last, 0)

    block = score_part.shape[1]
    score_copies = scatter(score_part, score_recv, line, score_send, score_got)
    for d in list(range(1, n)) + [0]:
        peer = lax.rem(coord + d, n)
        rows = projected[pl.ds(pl.multiple_of(peer * block, block), block), :]
        score_part[peer] = mix_rows(rows[:, :width], rows[:, width:], stacks.at[0])
        if d:
            score_copies[d - 1].start()

    def finish(c, carry):
        for h in range(2):
            basis_ref[h, rows_of(c)] = mix_rows(
                mixed[0, h, rows_of(c)], mixed[1, h, rows_of(c)], stacks.at[0]
            )
        return carry

    lax.fori_loop(0, chunks, finish, 0)
    scores_ref[...] = summed(score_part, score_recv, line, score_copies)

    sent(copies + gathered + low_copies + low_gathered + up_copies + up_gathered + score_copies)
    sent(map_copies + [across_swap, up_swap])
    for i in range(early):
        far_given(i).wait_send()
        far_mine(i).wait_send()
        ship(turn_of(upper, early + i)).wait_send()
    for c in range(chunks):
        give(c).wait_send()
        share(0, c).wait_send()
        share(1, c).wait_send()


def on_device(shapes, sketch_signs, merge_sketch):
    n = lax.axis_size("coord")
    _, subjects, coords = shapes.shape
    width = sketch_signs.shape[2]
    half = coords // 2
    tile = math.gcd(half // 2, 512)
    chunks = half // tile
    rows = subjects // n
    line = (n, width // n, width)
    pair = (2 * n, width // (2 * n), width)
    vmem, dma = pltpu.VMEM, pltpu.SemaphoreType.DMA
    basis, scores = pl.pallas_call(
        functools.partial(whole_kernel, n, tile),
        out_shape=(
            jax.ShapeDtypeStruct((2, half, width), F32),
            jax.ShapeDtypeStruct((rows, width), F32),
        ),
        in_specs=[pl.BlockSpec(memory_space=pltpu.HBM)] * 3,
        out_specs=(pl.BlockSpec(memory_space=vmem), pl.BlockSpec(memory_space=vmem)),
        scratch_shapes=[
            vmem((2 * chunks, subjects, tile), BF16),
            vmem((subjects, width), jnp.int32),
            vmem(merge_sketch.shape, F32),
            vmem((width, subjects), BF16),
            vmem((half, width), F32),
            vmem((2, half, width), F32),
            vmem((2, chunks // 2, tile, width), F32),
            vmem((2, 2, half, width), F32),
            vmem((2, 6 * width, width), BF16),
            vmem((2, 2, width, width), F32),
            vmem((2, width, width), F32),
            vmem((2, width, width), F32),
            vmem((width, width), F32),
            vmem((width, 2 * width), F32),
            vmem((width, width), F32),
            vmem((subjects, 2 * width), F32),
        ]
        + [vmem(line, F32)] * 3
        + [vmem(pair, F32)] * 6
        + [
            vmem((2,) + pair[1:], F32),
            vmem((n, rows, width), F32),
            vmem((n, rows, width), F32),
            dma((2, chunks)),
            dma((2,)),
        ]
        + [dma((chunks,))] * 2
        + [dma((2, chunks // 2))] * 2
        + [dma((2, chunks))] * 2
        + [dma((chunks,))] * 2
        + [dma((n,))] * 6
        + [dma((2 * n,))] * 8
        + [dma((5,))] * 2,
        compiler_params=pltpu.CompilerParams(
            collective_id=0, has_side_effects=True, vmem_limit_bytes=48 * 1024 * 1024
        ),
        name="shape_pca",
    )(
        shapes[0],
        pltpu.with_memory_space_constraint(sketch_signs[0], pltpu.HBM),
        pltpu.with_memory_space_constraint(merge_sketch, pltpu.HBM),
    )
    total_coords = coords * n
    basis = basis.reshape(coords, width) * math.sqrt(total_coords)
    scores = scores * (4.0 * math.sqrt(width / total_coords))
    return basis[None], scores[None]


def solution(mesh):
    placed = (P("cohort", None, "coord"), P("cohort", None, None), P())
    return jax.shard_map(
        on_device,
        mesh=mesh,
        in_specs=placed,
        out_specs=(P("cohort", "coord", None), P("cohort", "coord", None)),
        check_vma=False,
    )
```

```python
import functools
import math

import jax
import jax.numpy as jnp
from jax import lax
from jax.experimental import pallas as pl
from jax.experimental.pallas import tpu as pltpu
from jax.sharding import PartitionSpec as P

HIGHEST = lax.Precision.HIGHEST
MESH = pl.DeviceIdType.MESH
F32 = jnp.float32
BF16 = jnp.bfloat16


def dot(a, b):
    return jnp.dot(a, b, preferred_element_type=F32)


def dot_high(a, b, dims):
    return lax.dot_general(a, b, (dims, ((), ())), precision=HIGHEST, preferred_element_type=F32)


def split(x):
    high = x.astype(BF16)
    return high, (x - high.astype(F32)).astype(BF16)


def cross_product(a, b):
    dims = (((0,), (0,)), ((), ()))
    a_high, a_mid = split(a)
    b_high, b_mid = split(b)
    wide = lax.dot_general(
        a_high, jnp.concatenate([b_high, b_mid], axis=1), dims, preferred_element_type=F32
    )
    width = b.shape[1]
    return (
        wide[:, :width]
        + wide[:, width:]
        + lax.dot_general(a_mid, b_high, dims, preferred_element_type=F32)
    )


def stack_map(stacked, which, value):
    high, mid = split(value)
    width = value.shape[0]
    base = 3 * width * which
    stacked[base : base + width, :] = high
    stacked[base + width : base + 2 * width, :] = high
    stacked[base + 2 * width : base + 3 * width, :] = mid


def mix_rows(low, up, stacked):
    low_high, low_mid = split(low)
    up_high, up_mid = split(up)
    rows = jnp.concatenate([low_high, low_mid, low_high, up_high, up_mid, up_high], axis=1)
    return dot(rows, stacked[...])


def inverse_of(gram, x_ref):
    size = gram.shape[1]
    step = 8
    tiles = size // step
    lane = lax.broadcasted_iota(jnp.int32, (step, size), 1)
    sub = lax.broadcasted_iota(jnp.int32, (step, size), 0)

    def full(x):
        return jnp.broadcast_to(x, (step, size))

    def total(terms):
        while len(terms) > 1:
            terms = [terms[i] + terms[i + 1] for i in range(0, len(terms), 2)]
        return terms[0]

    both = [gram[t * step : (t + 1) * step, :] for t in range(tiles)]
    for t in range(tiles):
        at = t * step
        inside = (lane >= at) & (lane < at + step)
        cols = [full(both[t][:, at + k : at + k + 1]) for k in range(step)]
        e = [[full(cols[k][i : i + 1, :]) for k in range(i + 1)] for i in range(step)]
        head = jnp.where(inside, (lane - at == sub).astype(F32), both[t])
        rows = [full(head[i : i + 1, :]) for i in range(step)]
        f = {}
        inv = []
        for s in range(step):
            inv.append(1.0 / e[s][s])
            for i in range(s + 1, step):
                f[i, s] = e[i][s] * inv[s]
                for k in range(s + 1, i + 1):
                    e[i][k] = e[i][k] - f[i, s] * e[k][s]
            for i in range(s + 1, step):
                rows[i] = rows[i] - f[i, s] * rows[s]
        out = rows[0] * lax.rsqrt(e[0][0])
        for s in range(1, step):
            out = jnp.where(sub == s, rows[s] * lax.rsqrt(e[s][s]), out)
        x_ref[at : at + step, :] = jnp.where(lane < at + step, out, 0.0)
        rows = [rows[s] * inv[s] for s in range(step)]
        for u in range(t + 1, tiles):
            c = [full(both[u][:, at + s : at + s + 1]) for s in range(step)]
            for s in range(step):
                for r in range(s):
                    c[s] = c[s] - f[s, r] * c[r]
            both[u] = jnp.where(inside, 0.0, both[u]) - total([c[s] * rows[s] for s in range(step)])


def remote(src, dst, send, got, device):
    return pltpu.make_async_remote_copy(
        src_ref=src, dst_ref=dst, send_sem=send, recv_sem=got, device_id=device, device_id_type=MESH
    )


def scatter(part, recv, group, send, got):
    me, size, ident = group
    copies = []
    for d in range(1, size):
        peer = lax.rem(me + d, size)
        copies.append(remote(part.at[peer], recv.at[d], send.at[d], got.at[d], ident(peer)))
    return copies


def start(copies):
    for copy in copies:
        copy.start()


def summed(part, recv, group, copies):
    me, size, ident = group
    total = part[me]
    for d in range(1, size):
        copies[d - 1].wait_recv()
        total = total + recv[d]
    return total


def spread(out, group, send, got):
    me, size, ident = group
    return [
        remote(out.at[me], out.at[me], send.at[d], got.at[d], ident(lax.rem(me + d, size)))
        for d in range(1, size)
    ]


def received(copies):
    for copy in copies:
        copy.wait_recv()


def sent(copies):
    for copy in copies:
        copy.wait_send()


def whole_kernel(
    n, tile, scale, grow, shapes_ref, signs_ref, merge_ref, basis_ref, scores_ref,
    held, signs, merge, turned, given, pairs, far, mixed, stacks, low_maps, up_maps, outer, x_ref,
    flats, parts, wide, products, projected, gram_part, gram_recv, gram, low_part, low_recv, low_gram,
    up_part, up_recv, up_gram, up_other, score_part, score_recv,
    loaded, small, give_send, give_got, far_send, far_got, core_send, core_got,
    cross_send, cross_got, gram_send, gram_got, gram_send2, gram_got2, score_send, score_got,
    low_send, low_got, low_send2, low_got2, up_send, up_got, up_send2, up_got2, map_send, map_got,
):
    coord = lax.axis_index("coord")
    cohort = lax.axis_index("cohort")
    side = lax.rem(cohort, 2)
    upper = lax.rem(cohort // 2, 2)
    base = cohort - side
    partner = {"cohort": cohort + 1 - 2 * side}
    across = {"cohort": cohort + 2 - 4 * upper}
    corner = {"cohort": cohort + 2 - 4 * upper + 1 - 2 * side}
    line = (coord, n, lambda r: {"coord": r})
    pair = (
        coord * 2 + side, 2 * n, lambda r: {"coord": r // 2, "cohort": base + lax.rem(r, 2)}
    )
    chunks = held.shape[0] // 2
    early = chunks // 2
    width = turned.shape[0]

    def rows_of(c):
        return pl.ds(pl.multiple_of(c * tile, tile), tile)

    def turn_of(which, i):
        return lax.rem(i + which * early, chunks)

    small_copies = [
        pltpu.make_async_copy(signs_ref, signs, small.at[0]),
        pltpu.make_async_copy(merge_ref, merge, small.at[1]),
    ]
    start(small_copies)

    def load(j):
        h = side if j % 2 else 1 - side
        at = pl.multiple_of((h * chunks + turn_of(upper, j // 2)) * tile, tile)
        return pltpu.make_async_copy(shapes_ref.at[:, pl.ds(at, tile)], held.at[j], loaded.at[j])

    for j in range(2 * chunks):
        load(j).start()

    barrier = pltpu.get_barrier_semaphore()
    me, size, ident = pair
    for d in range(1, size):
        pl.semaphore_signal(
            barrier, inc=1, device_id=ident(lax.rem(me + d, size)), device_id_type=MESH
        )
    pl.semaphore_signal(barrier, inc=1, device_id=across, device_id_type=MESH)
    pl.semaphore_signal(barrier, inc=1, device_id=corner, device_id_type=MESH)
    wide[...] = jnp.zeros_like(wide)
    products[...] = jnp.zeros_like(products)

    def give(c):
        return remote(
            given.at[rows_of(c)], pairs.at[side, rows_of(c)], give_send.at[c], give_got.at[c], partner
        )

    def far_given(i):
        return remote(
            given.at[rows_of(turn_of(upper, i))], far.at[side, i],
            far_send.at[0, i], far_got.at[0, i], corner,
        )

    def far_mine(i):
        return remote(
            pairs.at[side, rows_of(turn_of(upper, i))], far.at[side, i],
            far_send.at[1, i], far_got.at[1, i], across,
        )

    def center(j):
        load(j).wait()
        block = held.at[j]
        mean = jnp.sum(block[...].astype(F32), axis=0, keepdims=True) * (1.0 / block.shape[0])
        block[...] = (block[...].astype(F32) - mean).astype(BF16)

    def sketch(j):
        flat = dot(turned[...], held[j])
        rows = flat.T
        if j % 2:
            pairs[side, rows_of(turn_of(upper, j // 2))] = rows
        else:
            given[rows_of(turn_of(upper, j // 2))] = rows
        high, mid = split(rows)
        flats[j % 2] = flat.astype(BF16)
        parts[j % 2, :, :width] = high
        parts[j % 2, :, width:] = mid

    def send_sketch(j):
        i = j // 2
        if i < early:
            (far_mine(i) if j % 2 else far_given(i)).start()
        if j % 2 == 0:
            give(turn_of(upper, i)).start()

    center(0)
    small_copies[0].wait()
    turned[...] = signs[...].astype(F32).T.astype(BF16)
    for j in range(2 * chunks):
        if j + 1 < 2 * chunks:
            center(j + 1)
        sketch(j)
        if j:
            wide[...] += dot(flats[(j - 1) % 2], parts[(j - 1) % 2])
        else:
            pl.semaphore_wait(barrier, size + 1)
        send_sketch(j)
    wide[...] += dot(flats[1], parts[1])
    turn = wide[:, width:]
    own = wide[:, :width] + turn + turn.T
    gram_part[...] = own.reshape(gram_part.shape)
    copies = scatter(gram_part, gram_recv, line, gram_send, gram_got)
    start(copies)

    def cross(i, carry):
        c = turn_of(upper, i)
        give(c).wait_recv()
        products[...] += cross_product(pairs[0, rows_of(c)], pairs[1, rows_of(c)])
        return carry

    lax.fori_loop(0, chunks, cross, 0)
    low_part[...] = products[...].reshape(low_part.shape)
    gram[coord] = summed(gram_part, gram_recv, line, copies)
    gathered = spread(gram, line, gram_send2, gram_got2)
    start(gathered)
    low_copies = scatter(low_part, low_recv, pair, low_send, low_got)
    start(low_copies)
    small_copies[1].wait()
    for l in range(2):
        outer[l] = dot_high(merge[l, 0], merge[l, 0], ((0,), (0,))) + dot_high(
            merge[l, 1], merge[l, 1], ((0,), (0,))
        )
    received(gathered)

    inverse_of(gram[...].reshape(width, width), x_ref)
    low_maps[upper, side] = dot_high(x_ref[...], merge[0, side], ((0,), (0,)))
    own_map = low_maps.at[upper, side]
    map_copies = [
        remote(own_map, own_map, map_send.at[i], map_got.at[i], device)
        for i, device in enumerate((partner, across, corner))
    ]
    start(map_copies)
    low_gram[pair[0]] = summed(low_part, low_recv, pair, low_copies)
    low_gathered = spread(low_gram, pair, low_send2, low_got2)
    start(low_gathered)
    map_copies[0].wait_recv()
    for i in range(2):
        stack_map(stacks.at[0], i, low_maps[upper, i])

    def ship(c):
        rows = mixed.at[upper, side, rows_of(c)]
        return remote(rows, rows, cross_send.at[c], cross_got.at[c], across)

    def share(which, c):
        far_side = lax.rem(which + upper, 2)
        rows = mixed.at[far_side, side, rows_of(c)]
        return remote(rows, rows, core_send.at[which, c], core_got.at[which, c], partner)

    def blend(i):
        c = turn_of(upper, i)
        mixed[upper, side, rows_of(c)] = mix_rows(
            pairs[0, rows_of(c)], pairs[1, rows_of(c)], stacks.at[0]
        )
        share(0, c).start()
        return c

    for i in range(early, chunks):
        ship(blend(i)).start()
    for i in range(early):
        blend(i)
    received(map_copies[1:])
    for i in range(2):
        stack_map(stacks.at[1], i, low_maps[1 - upper, i])

    products[...] = jnp.zeros_like(products)

    def meet(i, carry):
        c = turn_of(1 - upper, i)
        far_given(i).wait_recv()
        far_mine(i).wait_recv()
        mixed[1 - upper, side, rows_of(c)] = mix_rows(far[0, i], far[1, i], stacks.at[1])
        share(1, c).start()
        products[...] += cross_product(mixed[0, side, rows_of(c)], mixed[1, side, rows_of(c)])
        return carry

    lax.fori_loop(0, early, meet, 0)
    up_part[...] = products[...].reshape(up_part.shape)
    up_copies = scatter(up_part, up_recv, pair, up_send, up_got)
    start(up_copies)
    received(low_gathered)
    inner = dot_high(
        low_maps[upper, 0],
        dot_high(low_gram[...].reshape(width, width), low_maps[upper, 1], ((1,), (0,))),
        ((0,), (0,)),
    )
    inverse_of(outer[0] + inner + inner.T, x_ref)
    up_maps[upper] = dot_high(x_ref[...], merge[1, upper], ((0,), (0,)))
    up_other[upper] = summed(up_part, up_recv, pair, up_copies)
    up_swap = remote(up_other.at[upper], up_other.at[upper], map_send.at[3], map_got.at[3], across)
    up_swap.start()
    across_swap = remote(
        up_maps.at[upper], up_maps.at[upper], map_send.at[4], map_got.at[4], across
    )
    across_swap.start()

    projected[...] = jnp.zeros_like(projected)

    def project(h, i):
        c = turn_of(1 - upper, i)
        rows = jnp.concatenate(
            [mixed[0, h, rows_of(c)].astype(BF16), mixed[1, h, rows_of(c)].astype(BF16)], axis=1
        )
        place = 2 * lax.rem(i + early, chunks) + lax.rem(h + side + 1, 2)
        projected[...] += dot(held[place], rows)

    def project_given(i):
        c = turn_of(1 - upper, i)
        share(0, c).wait_recv()
        share(1, c).wait_recv()
        project(1 - side, i)

    def project_early(i, carry):
        project(side, i)
        project_given(i)
        return carry

    def project_late(i, carry):
        c = turn_of(1 - upper, i)
        ship(c).wait_recv()
        share(1, c).start()
        project(side, i)
        return carry

    def project_last(i, carry):
        project_given(i)
        return carry

    lax.fori_loop(0, 1, project_early, 0)
    up_swap.wait_recv()
    up_gram[pair[0]] = up_other[0] + up_other[1]
    up_gathered = spread(up_gram, pair, up_send2, up_got2)
    start(up_gathered)
    lax.fori_loop(1, early, project_early, 0)
    lax.fori_loop(early, chunks, project_late, 0)
    across_swap.wait_recv()
    received(up_gathered)
    inner = dot_high(
        up_maps[0],
        dot_high(up_gram[...].reshape(width, width), up_maps[1], ((1,), (0,))),
        ((0,), (0,)),
    )
    inverse_of(outer[1] + inner + inner.T, x_ref)
    for i in range(2):
        last = dot_high(up_maps[i], x_ref[...], ((1,), (1,)))
        stack_map(stacks.at[0], i, last * scale)
        stack_map(stacks.at[1], i, last * grow)
    lax.fori_loop(early, chunks, project_last, 0)

    block = score_part.shape[1]
    score_copies = scatter(score_part, score_recv, line, score_send, score_got)
    for d in list(range(1, n)) + [0]:
        peer = lax.rem(coord + d, n)
        rows = projected[pl.ds(pl.multiple_of(peer * block, block), block), :]
        score_part[peer] = mix_rows(rows[:, :width], rows[:, width:], stacks.at[0])
        if d:
            score_copies[d - 1].start()

    def finish(c, carry):
        for h in range(2):
            basis_ref[h, rows_of(c)] = mix_rows(
                mixed[0, h, rows_of(c)], mixed[1, h, rows_of(c)], stacks.at[1]
            )
        return carry

    lax.fori_loop(0, chunks, finish, 0)
    scores_ref[...] = summed(score_part, score_recv, line, score_copies)

    sent(copies + gathered + low_copies + low_gathered + up_copies + up_gathered + score_copies)
    sent(map_copies + [across_swap, up_swap])
    for i in range(early):
        far_given(i).wait_send()
        far_mine(i).wait_send()
        ship(turn_of(upper, early + i)).wait_send()
    for c in range(chunks):
        give(c).wait_send()
        share(0, c).wait_send()
        share(1, c).wait_send()


def store_kernel(basis_ref, scores_ref, basis_out, scores_out, sems):
    copies = [
        pltpu.make_async_copy(basis_ref.at[h], basis_out.at[h], sems.at[h]) for h in range(2)
    ]
    copies.append(pltpu.make_async_copy(scores_ref, scores_out, sems.at[2]))
    start(copies)
    for copy in copies:
        copy.wait()


def on_device(shapes, sketch_signs, merge_sketch):
    n = lax.axis_size("coord")
    _, subjects, coords = shapes.shape
    width = sketch_signs.shape[2]
    half = coords // 2
    tile = math.gcd(half // 2, 512)
    chunks = half // tile
    rows = subjects // n
    line = (n, width // n, width)
    pair = (2 * n, width // (2 * n), width)
    scale = 4.0 * math.sqrt(width / (coords * n))
    grow = math.sqrt(coords * n)
    vmem, dma = pltpu.VMEM, pltpu.SemaphoreType.DMA
    basis, scores = pl.pallas_call(
        functools.partial(whole_kernel, n, tile, scale, grow),
        out_shape=(
            jax.ShapeDtypeStruct((2, half, width), F32),
            jax.ShapeDtypeStruct((rows, width), F32),
        ),
        in_specs=[pl.BlockSpec(memory_space=pltpu.HBM)] * 3,
        out_specs=(pl.BlockSpec(memory_space=vmem), pl.BlockSpec(memory_space=vmem)),
        scratch_shapes=[
            vmem((2 * chunks, subjects, tile), BF16),
            vmem((subjects, width), jnp.int32),
            vmem(merge_sketch.shape, F32),
            vmem((width, subjects), BF16),
            vmem((half, width), F32),
            vmem((2, half, width), F32),
            vmem((2, chunks // 2, tile, width), F32),
            vmem((2, 2, half, width), F32),
            vmem((2, 6 * width, width), BF16),
            vmem((2, 2, width, width), F32),
            vmem((2, width, width), F32),
            vmem((2, width, width), F32),
            vmem((width, width), F32),
            vmem((2, width, tile), BF16),
            vmem((2, tile, 2 * width), BF16),
            vmem((width, 2 * width), F32),
            vmem((width, width), F32),
            vmem((subjects, 2 * width), F32),
        ]
        + [vmem(line, F32)] * 3
        + [vmem(pair, F32)] * 6
        + [
            vmem((2,) + pair[1:], F32),
            vmem((n, rows, width), F32),
            vmem((n, rows, width), F32),
            dma((2 * chunks,)),
            dma((2,)),
        ]
        + [dma((chunks,))] * 2
        + [dma((2, chunks // 2))] * 2
        + [dma((2, chunks))] * 2
        + [dma((chunks,))] * 2
        + [dma((n,))] * 6
        + [dma((2 * n,))] * 8
        + [dma((5,))] * 2,
        compiler_params=pltpu.CompilerParams(
            collective_id=0, has_side_effects=True, vmem_limit_bytes=48 * 1024 * 1024
        ),
        name="shape_pca",
    )(
        shapes[0],
        pltpu.with_memory_space_constraint(sketch_signs[0], pltpu.HBM),
        pltpu.with_memory_space_constraint(merge_sketch, pltpu.HBM),
    )
    basis, scores = pl.pallas_call(
        store_kernel,
        out_shape=(
            jax.ShapeDtypeStruct(basis.shape, F32),
            jax.ShapeDtypeStruct(scores.shape, F32),
        ),
        in_specs=[pl.BlockSpec(memory_space=vmem)] * 2,
        out_specs=(pl.BlockSpec(memory_space=pltpu.HBM),) * 2,
        scratch_shapes=[dma((3,))],
        name="store",
    )(
        pltpu.with_memory_space_constraint(basis, pltpu.VMEM),
        pltpu.with_memory_space_constraint(scores, pltpu.VMEM),
    )
    return basis.reshape(1, coords, width), scores[None]


def solution(mesh):
    placed = (P("cohort", None, "coord"), P("cohort", None, None), P())
    return jax.shard_map(
        on_device,
        mesh=mesh,
        in_specs=placed,
        out_specs=(P("cohort", "coord", None), P("cohort", "coord", None)),
        check_vma=False,
    )
```

```python
import functools
import math

import jax
import jax.numpy as jnp
from jax import lax
from jax.experimental import pallas as pl
from jax.experimental.pallas import tpu as pltpu
from jax.sharding import PartitionSpec as P

HIGHEST = lax.Precision.HIGHEST
MESH = pl.DeviceIdType.MESH
F32 = jnp.float32
BF16 = jnp.bfloat16


def dot(a, b):
    return jnp.dot(a, b, preferred_element_type=F32)


def dot_high(a, b, dims):
    return lax.dot_general(a, b, (dims, ((), ())), precision=HIGHEST, preferred_element_type=F32)


def split(x):
    high = x.astype(BF16)
    return high, (x - high.astype(F32)).astype(BF16)


def cross_product(a, b):
    dims = (((0,), (0,)), ((), ()))
    a_high, a_mid = split(a)
    b_high, b_mid = split(b)
    wide = lax.dot_general(
        a_high, jnp.concatenate([b_high, b_mid], axis=1), dims, preferred_element_type=F32
    )
    width = b.shape[1]
    return (
        wide[:, :width]
        + wide[:, width:]
        + lax.dot_general(a_mid, b_high, dims, preferred_element_type=F32)
    )


def stack_map(stacked, which, value):
    high, mid = split(value)
    width = value.shape[0]
    base = 3 * width * which
    stacked[base : base + width, :] = high
    stacked[base + width : base + 2 * width, :] = high
    stacked[base + 2 * width : base + 3 * width, :] = mid


def mix_rows(low, up, stacked):
    low_high, low_mid = split(low)
    up_high, up_mid = split(up)
    rows = jnp.concatenate([low_high, low_mid, low_high, up_high, up_mid, up_high], axis=1)
    return dot(rows, stacked[...])


def inverse_of(gram, x_ref):
    size = gram.shape[1]
    step = 8
    tiles = size // step
    lane = lax.broadcasted_iota(jnp.int32, (step, size), 1)
    sub = lax.broadcasted_iota(jnp.int32, (step, size), 0)

    def full(x):
        return jnp.broadcast_to(x, (step, size))

    def total(terms):
        while len(terms) > 1:
            terms = [terms[i] + terms[i + 1] for i in range(0, len(terms), 2)]
        return terms[0]

    both = [gram[t * step : (t + 1) * step, :] for t in range(tiles)]
    for t in range(tiles):
        at = t * step
        inside = (lane >= at) & (lane < at + step)
        cols = [full(both[t][:, at + k : at + k + 1]) for k in range(step)]
        e = [[full(cols[k][i : i + 1, :]) for k in range(i + 1)] for i in range(step)]
        head = jnp.where(inside, (lane - at == sub).astype(F32), both[t])
        rows = [full(head[i : i + 1, :]) for i in range(step)]
        f = {}
        inv = []
        for s in range(step):
            inv.append(1.0 / e[s][s])
            for i in range(s + 1, step):
                f[i, s] = e[i][s] * inv[s]
                for k in range(s + 1, i + 1):
                    e[i][k] = e[i][k] - f[i, s] * e[k][s]
            for i in range(s + 1, step):
                rows[i] = rows[i] - f[i, s] * rows[s]
        out = rows[0] * lax.rsqrt(e[0][0])
        for s in range(1, step):
            out = jnp.where(sub == s, rows[s] * lax.rsqrt(e[s][s]), out)
        x_ref[at : at + step, :] = jnp.where(lane < at + step, out, 0.0)
        rows = [rows[s] * inv[s] for s in range(step)]
        for u in range(t + 1, tiles):
            c = [full(both[u][:, at + s : at + s + 1]) for s in range(step)]
            for s in range(step):
                for r in range(s):
                    c[s] = c[s] - f[s, r] * c[r]
            both[u] = jnp.where(inside, 0.0, both[u]) - total([c[s] * rows[s] for s in range(step)])


def remote(src, dst, send, got, device):
    return pltpu.make_async_remote_copy(
        src_ref=src, dst_ref=dst, send_sem=send, recv_sem=got, device_id=device, device_id_type=MESH
    )


def scatter(part, recv, group, send, got):
    me, size, ident = group
    copies = []
    for d in range(1, size):
        peer = lax.rem(me + d, size)
        copies.append(remote(part.at[peer], recv.at[d], send.at[d], got.at[d], ident(peer)))
    return copies


def start(copies):
    for copy in copies:
        copy.start()


def summed(part, recv, group, copies):
    me, size, ident = group
    total = part[me]
    for d in range(1, size):
        copies[d - 1].wait_recv()
        total = total + recv[d]
    return total


def spread(out, group, send, got):
    me, size, ident = group
    return [
        remote(out.at[me], out.at[me], send.at[d], got.at[d], ident(lax.rem(me + d, size)))
        for d in range(1, size)
    ]


def received(copies):
    for copy in copies:
        copy.wait_recv()


def sent(copies):
    for copy in copies:
        copy.wait_send()


def whole_kernel(
    n, tile, scale, grow, shapes_ref, signs_ref, merge_ref, basis_ref, scores_ref,
    held, signs, merge, turned, given, pairs, far, mixed, stacks, low_maps, up_maps, outer, x_ref,
    flats, parts, wide, products, projected, gram_part, gram_recv, gram, low_part, low_recv, low_gram,
    up_part, up_recv, up_gram, up_other, score_part, score_recv,
    loaded, small, give_send, give_got, far_send, far_got, core_send, core_got,
    cross_send, cross_got, gram_send, gram_got, gram_send2, gram_got2, score_send, score_got,
    low_send, low_got, low_send2, low_got2, up_send, up_got, up_send2, up_got2, map_send, map_got,
):
    coord = lax.axis_index("coord")
    cohort = lax.axis_index("cohort")
    side = lax.rem(cohort, 2)
    upper = lax.rem(cohort // 2, 2)
    base = cohort - side
    partner = {"cohort": cohort + 1 - 2 * side}
    across = {"cohort": cohort + 2 - 4 * upper}
    corner = {"cohort": cohort + 2 - 4 * upper + 1 - 2 * side}
    line = (coord, n, lambda r: {"coord": r})
    pair = (
        coord * 2 + side, 2 * n, lambda r: {"coord": r // 2, "cohort": base + lax.rem(r, 2)}
    )
    chunks = held.shape[0] // 2
    early = chunks // 2
    piece = tile // 2
    raw = far.shape[1]
    width = turned.shape[0]

    def rows_of(c):
        return pl.ds(pl.multiple_of(c * tile, tile), tile)

    def piece_of(which, p):
        at = turn_of(which, p // 2) * tile + (p % 2) * piece
        return pl.ds(pl.multiple_of(at, piece), piece)

    def turn_of(which, i):
        return lax.rem(i + which * early, chunks)

    small_copies = [
        pltpu.make_async_copy(signs_ref, signs, small.at[0]),
        pltpu.make_async_copy(merge_ref, merge, small.at[1]),
    ]
    start(small_copies)

    def load(j):
        h = side if j % 2 else 1 - side
        at = pl.multiple_of((h * chunks + turn_of(upper, j // 2)) * tile, tile)
        return pltpu.make_async_copy(shapes_ref.at[:, pl.ds(at, tile)], held.at[j], loaded.at[j])

    for j in range(3):
        load(j).start()

    barrier = pltpu.get_barrier_semaphore()
    me, size, ident = pair
    for d in range(1, size):
        pl.semaphore_signal(
            barrier, inc=1, device_id=ident(lax.rem(me + d, size)), device_id_type=MESH
        )
    pl.semaphore_signal(barrier, inc=1, device_id=across, device_id_type=MESH)
    pl.semaphore_signal(barrier, inc=1, device_id=corner, device_id_type=MESH)
    wide[...] = jnp.zeros_like(wide)
    products[...] = jnp.zeros_like(products)

    def give(c):
        return remote(
            given.at[rows_of(c)], pairs.at[side, rows_of(c)], give_send.at[c], give_got.at[c], partner
        )

    def far_given(p):
        return remote(
            given.at[piece_of(upper, p)], far.at[side, p], far_send.at[0, p], far_got.at[0, p], corner
        )

    def far_mine(p):
        return remote(
            pairs.at[side, piece_of(upper, p)], far.at[side, p],
            far_send.at[1, p], far_got.at[1, p], across,
        )

    def center(j):
        load(j).wait()
        if j + 3 < 2 * chunks:
            load(j + 3).start()
        block = held.at[j]
        mean = jnp.sum(block[...].astype(F32), axis=0, keepdims=True) * (1.0 / block.shape[0])
        block[...] = (block[...].astype(F32) - mean).astype(BF16)

    def sketch(j):
        flat = dot(turned[...], held[j])
        rows = flat.T
        if j % 2:
            pairs[side, rows_of(turn_of(upper, j // 2))] = rows
        else:
            given[rows_of(turn_of(upper, j // 2))] = rows
        high, mid = split(rows)
        flats[j % 2] = flat.astype(BF16)
        parts[j % 2, :, :width] = high
        parts[j % 2, :, width:] = mid

    def send_sketch(j):
        i = j // 2
        for p in range(2 * i, min(2 * i + 2, raw)):
            (far_mine(p) if j % 2 else far_given(p)).start()
        if j % 2 == 0:
            give(turn_of(upper, i)).start()

    center(0)
    small_copies[0].wait()
    turned[...] = signs[...].astype(F32).T.astype(BF16)
    for j in range(2 * chunks):
        if j + 1 < 2 * chunks:
            center(j + 1)
        sketch(j)
        if j:
            wide[...] += dot(flats[(j - 1) % 2], parts[(j - 1) % 2])
        else:
            pl.semaphore_wait(barrier, size + 1)
        send_sketch(j)
    wide[...] += dot(flats[1], parts[1])
    turn = wide[:, width:]
    own = wide[:, :width] + turn + turn.T
    gram_part[...] = own.reshape(gram_part.shape)
    copies = scatter(gram_part, gram_recv, line, gram_send, gram_got)
    start(copies)

    def cross(i, carry):
        c = turn_of(upper, i)
        give(c).wait_recv()
        products[...] += cross_product(pairs[0, rows_of(c)], pairs[1, rows_of(c)])
        return carry

    lax.fori_loop(0, chunks, cross, 0)
    low_part[...] = products[...].reshape(low_part.shape)
    gram[coord] = summed(gram_part, gram_recv, line, copies)
    gathered = spread(gram, line, gram_send2, gram_got2)
    start(gathered)
    low_copies = scatter(low_part, low_recv, pair, low_send, low_got)
    start(low_copies)
    small_copies[1].wait()
    for l in range(2):
        outer[l] = dot_high(merge[l, 0], merge[l, 0], ((0,), (0,))) + dot_high(
            merge[l, 1], merge[l, 1], ((0,), (0,))
        )
    received(gathered)

    inverse_of(gram[...].reshape(width, width), x_ref)
    low_maps[upper, side] = dot_high(x_ref[...], merge[0, side], ((0,), (0,)))
    own_map = low_maps.at[upper, side]
    map_copies = [
        remote(own_map, own_map, map_send.at[i], map_got.at[i], device)
        for i, device in enumerate((partner, across, corner))
    ]
    start(map_copies)
    low_gram[pair[0]] = summed(low_part, low_recv, pair, low_copies)
    low_gathered = spread(low_gram, pair, low_send2, low_got2)
    start(low_gathered)
    map_copies[0].wait_recv()
    for i in range(2):
        stack_map(stacks.at[0], i, low_maps[upper, i])

    def ship(which, p):
        rows = mixed.at[which, side, piece_of(which, p)]
        return remote(rows, rows, cross_send.at[p], cross_got.at[p], across)

    def share(which, c):
        far_side = lax.rem(which + upper, 2)
        rows = mixed.at[far_side, side, rows_of(c)]
        return remote(rows, rows, core_send.at[which, c], core_got.at[which, c], partner)

    def blend(i):
        c = turn_of(upper, i)
        mixed[upper, side, rows_of(c)] = mix_rows(
            pairs[0, rows_of(c)], pairs[1, rows_of(c)], stacks.at[0]
        )
        share(0, c).start()
        return c

    for i in list(range(raw // 2, chunks)) + list(range(raw // 2)):
        blend(i)
        for p in range(max(2 * i, raw), 2 * i + 2):
            ship(upper, p).start()
    received(map_copies[1:])
    for i in range(2):
        stack_map(stacks.at[1], i, low_maps[1 - upper, i])

    products[...] = jnp.zeros_like(products)

    for p in range(2 * early):
        c = turn_of(1 - upper, p // 2)
        rows = piece_of(1 - upper, p)
        if p < raw:
            far_given(p).wait_recv()
            far_mine(p).wait_recv()
            mixed[1 - upper, side, rows] = mix_rows(far[0, p], far[1, p], stacks.at[1])
        else:
            ship(1 - upper, p).wait_recv()
        if p % 2:
            share(1, c).start()
        products[...] += cross_product(mixed[0, side, rows], mixed[1, side, rows])
    up_part[...] = products[...].reshape(up_part.shape)
    up_copies = scatter(up_part, up_recv, pair, up_send, up_got)
    start(up_copies)
    received(low_gathered)
    inner = dot_high(
        low_maps[upper, 0],
        dot_high(low_gram[...].reshape(width, width), low_maps[upper, 1], ((1,), (0,))),
        ((0,), (0,)),
    )
    inverse_of(outer[0] + inner + inner.T, x_ref)
    up_maps[upper] = dot_high(x_ref[...], merge[1, upper], ((0,), (0,)))
    up_other[upper] = summed(up_part, up_recv, pair, up_copies)
    up_swap = remote(up_other.at[upper], up_other.at[upper], map_send.at[3], map_got.at[3], across)
    up_swap.start()
    across_swap = remote(
        up_maps.at[upper], up_maps.at[upper], map_send.at[4], map_got.at[4], across
    )
    across_swap.start()

    projected[...] = jnp.zeros_like(projected)

    def project(h, i):
        c = turn_of(1 - upper, i)
        rows = jnp.concatenate(
            [mixed[0, h, rows_of(c)].astype(BF16), mixed[1, h, rows_of(c)].astype(BF16)], axis=1
        )
        place = 2 * lax.rem(i + early, chunks) + lax.rem(h + side + 1, 2)
        projected[...] += dot(held[place], rows)

    def project_given(i):
        c = turn_of(1 - upper, i)
        share(0, c).wait_recv()
        share(1, c).wait_recv()
        project(1 - side, i)

    def project_early(i, carry):
        project(side, i)
        project_given(i)
        return carry

    lax.fori_loop(0, 1, project_early, 0)
    up_swap.wait_recv()
    up_gram[pair[0]] = up_other[0] + up_other[1]
    up_gathered = spread(up_gram, pair, up_send2, up_got2)
    start(up_gathered)
    lax.fori_loop(1, early, project_early, 0)
    for i in range(early, chunks):
        for p in range(2 * i, 2 * i + 2):
            ship(1 - upper, p).wait_recv()
        share(1, turn_of(1 - upper, i)).start()
        project(side, i)
    across_swap.wait_recv()
    for i in range(2):
        stack_map(stacks.at[0], i, up_maps[i])
    for i in range(early, chunks):
        project_given(i)

    block = score_part.shape[1]
    score_copies = scatter(score_part, score_recv, line, score_send, score_got)
    for d in list(range(1, n)) + [0]:
        peer = lax.rem(coord + d, n)
        rows = projected[pl.ds(pl.multiple_of(peer * block, block), block), :]
        score_part[peer] = mix_rows(rows[:, :width], rows[:, width:], stacks.at[0])
        if d:
            score_copies[d - 1].start()

    received(up_gathered)
    inner = dot_high(
        up_maps[0],
        dot_high(up_gram[...].reshape(width, width), up_maps[1], ((1,), (0,))),
        ((0,), (0,)),
    )
    inverse_of(outer[1] + inner + inner.T, x_ref)
    for i in range(2):
        stack_map(stacks.at[1], i, dot_high(up_maps[i], x_ref[...], ((1,), (1,))) * grow)

    def finish(c, carry):
        for h in range(2):
            basis_ref[h, rows_of(c)] = mix_rows(
                mixed[0, h, rows_of(c)], mixed[1, h, rows_of(c)], stacks.at[1]
            )
        return carry

    lax.fori_loop(0, chunks, finish, 0)
    total = summed(score_part, score_recv, line, score_copies)
    scores_ref[...] = dot_high(total, x_ref[...], ((1,), (1,))) * scale

    sent(copies + gathered + low_copies + low_gathered + up_copies + up_gathered + score_copies)
    sent(map_copies + [across_swap, up_swap])
    for p in range(2 * chunks):
        if p < raw:
            far_given(p).wait_send()
            far_mine(p).wait_send()
        else:
            ship(upper, p).wait_send()
    for c in range(chunks):
        give(c).wait_send()
        share(0, c).wait_send()
        share(1, c).wait_send()


def store_kernel(basis_ref, scores_ref, basis_out, scores_out, sems):
    copies = [
        pltpu.make_async_copy(basis_ref.at[h], basis_out.at[h], sems.at[h]) for h in range(2)
    ]
    copies.append(pltpu.make_async_copy(scores_ref, scores_out, sems.at[2]))
    start(copies)
    for copy in copies:
        copy.wait()


def on_device(shapes, sketch_signs, merge_sketch):
    n = lax.axis_size("coord")
    _, subjects, coords = shapes.shape
    width = sketch_signs.shape[2]
    half = coords // 2
    tile = math.gcd(half // 2, 512)
    chunks = half // tile
    raw = 3 * chunks // 4
    rows = subjects // n
    line = (n, width // n, width)
    pair = (2 * n, width // (2 * n), width)
    scale = 4.0 * math.sqrt(width / (coords * n))
    grow = math.sqrt(coords * n)
    vmem, dma = pltpu.VMEM, pltpu.SemaphoreType.DMA
    basis, scores = pl.pallas_call(
        functools.partial(whole_kernel, n, tile, scale, grow),
        out_shape=(
            jax.ShapeDtypeStruct((2, half, width), F32),
            jax.ShapeDtypeStruct((rows, width), F32),
        ),
        in_specs=[pl.BlockSpec(memory_space=pltpu.HBM)] * 3,
        out_specs=(pl.BlockSpec(memory_space=vmem), pl.BlockSpec(memory_space=vmem)),
        scratch_shapes=[
            vmem((2 * chunks, subjects, tile), BF16),
            vmem((subjects, width), jnp.int32),
            vmem(merge_sketch.shape, F32),
            vmem((width, subjects), BF16),
            vmem((half, width), F32),
            vmem((2, half, width), F32),
            vmem((2, raw, tile // 2, width), F32),
            vmem((2, 2, half, width), F32),
            vmem((2, 6 * width, width), BF16),
            vmem((2, 2, width, width), F32),
            vmem((2, width, width), F32),
            vmem((2, width, width), F32),
            vmem((width, width), F32),
            vmem((2, width, tile), BF16),
            vmem((2, tile, 2 * width), BF16),
            vmem((width, 2 * width), F32),
            vmem((width, width), F32),
            vmem((subjects, 2 * width), F32),
        ]
        + [vmem(line, F32)] * 3
        + [vmem(pair, F32)] * 6
        + [
            vmem((2,) + pair[1:], F32),
            vmem((n, rows, width), F32),
            vmem((n, rows, width), F32),
            dma((2 * chunks,)),
            dma((2,)),
        ]
        + [dma((chunks,))] * 2
        + [dma((2, raw))] * 2
        + [dma((2, chunks))] * 2
        + [dma((2 * chunks,))] * 2
        + [dma((n,))] * 6
        + [dma((2 * n,))] * 8
        + [dma((5,))] * 2,
        compiler_params=pltpu.CompilerParams(
            collective_id=0, has_side_effects=True, vmem_limit_bytes=48 * 1024 * 1024
        ),
        name="shape_pca",
    )(
        shapes[0],
        pltpu.with_memory_space_constraint(sketch_signs[0], pltpu.HBM),
        pltpu.with_memory_space_constraint(merge_sketch, pltpu.HBM),
    )
    basis, scores = pl.pallas_call(
        store_kernel,
        out_shape=(
            jax.ShapeDtypeStruct(basis.shape, F32),
            jax.ShapeDtypeStruct(scores.shape, F32),
        ),
        in_specs=[pl.BlockSpec(memory_space=vmem)] * 2,
        out_specs=(pl.BlockSpec(memory_space=pltpu.HBM),) * 2,
        scratch_shapes=[dma((3,))],
        name="store",
    )(
        pltpu.with_memory_space_constraint(basis, pltpu.VMEM),
        pltpu.with_memory_space_constraint(scores, pltpu.VMEM),
    )
    return basis.reshape(1, coords, width), scores[None]


def solution(mesh):
    placed = (P("cohort", None, "coord"), P("cohort", None, None), P())
    return jax.shard_map(
        on_device,
        mesh=mesh,
        in_specs=placed,
        out_specs=(P("cohort", "coord", None), P("cohort", "coord", None)),
        check_vma=False,
    )
```

```python
import functools
import math

import jax
import jax.numpy as jnp
from jax import lax
from jax.experimental import pallas as pl
from jax.experimental.pallas import tpu as pltpu
from jax.sharding import PartitionSpec as P

HIGHEST = lax.Precision.HIGHEST
MESH = pl.DeviceIdType.MESH
F32 = jnp.float32
BF16 = jnp.bfloat16


def dot(a, b):
    return jnp.dot(a, b, preferred_element_type=F32)


def dot_high(a, b, dims):
    return lax.dot_general(a, b, (dims, ((), ())), precision=HIGHEST, preferred_element_type=F32)


def split(x):
    high = x.astype(BF16)
    return high, (x - high.astype(F32)).astype(BF16)


def cross_product(a, b):
    dims = (((0,), (0,)), ((), ()))
    a_high, a_mid = split(a)
    b_high, b_mid = split(b)
    wide = lax.dot_general(
        a_high, jnp.concatenate([b_high, b_mid], axis=1), dims, preferred_element_type=F32
    )
    width = b.shape[1]
    return (
        wide[:, :width]
        + wide[:, width:]
        + lax.dot_general(a_mid, b_high, dims, preferred_element_type=F32)
    )


def stack_map(stacked, which, value):
    high, mid = split(value)
    width = value.shape[0]
    base = 3 * width * which
    stacked[base : base + width, :] = high
    stacked[base + width : base + 2 * width, :] = high
    stacked[base + 2 * width : base + 3 * width, :] = mid


def mix_rows(low, up, stacked):
    low_high, low_mid = split(low)
    up_high, up_mid = split(up)
    rows = jnp.concatenate([low_high, low_mid, low_high, up_high, up_mid, up_high], axis=1)
    return dot(rows, stacked[...])


def inverse_of(gram, x_ref, between=None):
    size = gram.shape[1]
    step = 8
    tiles = size // step
    lane = lax.broadcasted_iota(jnp.int32, (step, size), 1)
    sub = lax.broadcasted_iota(jnp.int32, (step, size), 0)

    def full(x):
        return jnp.broadcast_to(x, (step, size))

    def total(terms):
        while len(terms) > 1:
            terms = [terms[i] + terms[i + 1] for i in range(0, len(terms), 2)]
        return terms[0]

    both = [gram[t * step : (t + 1) * step, :] for t in range(tiles)]
    for t in range(tiles):
        at = t * step
        inside = (lane >= at) & (lane < at + step)
        cols = [full(both[t][:, at + k : at + k + 1]) for k in range(step)]
        e = [[full(cols[k][i : i + 1, :]) for k in range(i + 1)] for i in range(step)]
        head = jnp.where(inside, (lane - at == sub).astype(F32), both[t])
        rows = [full(head[i : i + 1, :]) for i in range(step)]
        f = {}
        inv = []
        for s in range(step):
            inv.append(1.0 / e[s][s])
            for i in range(s + 1, step):
                f[i, s] = e[i][s] * inv[s]
                for k in range(s + 1, i + 1):
                    e[i][k] = e[i][k] - f[i, s] * e[k][s]
            for i in range(s + 1, step):
                rows[i] = rows[i] - f[i, s] * rows[s]
        out = rows[0] * lax.rsqrt(e[0][0])
        for s in range(1, step):
            out = jnp.where(sub == s, rows[s] * lax.rsqrt(e[s][s]), out)
        x_ref[at : at + step, :] = jnp.where(lane < at + step, out, 0.0)
        rows = [rows[s] * inv[s] for s in range(step)]
        for u in range(t + 1, tiles):
            c = [full(both[u][:, at + s : at + s + 1]) for s in range(step)]
            for s in range(step):
                for r in range(s):
                    c[s] = c[s] - f[s, r] * c[r]
            both[u] = jnp.where(inside, 0.0, both[u]) - total([c[s] * rows[s] for s in range(step)])
        if between is not None:
            between(t, tiles)


def remote(src, dst, send, got, device):
    return pltpu.make_async_remote_copy(
        src_ref=src, dst_ref=dst, send_sem=send, recv_sem=got, device_id=device, device_id_type=MESH
    )


def scatter(part, recv, group, send, got):
    me, size, ident = group
    copies = []
    for d in range(1, size):
        peer = lax.rem(me + d, size)
        copies.append(remote(part.at[peer], recv.at[d], send.at[d], got.at[d], ident(peer)))
    return copies


def start(copies):
    for copy in copies:
        copy.start()


def summed(part, recv, group, copies):
    me, size, ident = group
    total = part[me]
    for d in range(1, size):
        copies[d - 1].wait_recv()
        total = total + recv[d]
    return total


def spread(out, group, send, got):
    me, size, ident = group
    return [
        remote(out.at[me], out.at[me], send.at[d], got.at[d], ident(lax.rem(me + d, size)))
        for d in range(1, size)
    ]


def received(copies):
    for copy in copies:
        copy.wait_recv()


def sent(copies):
    for copy in copies:
        copy.wait_send()


def whole_kernel(
    n, tile, scale, grow, shapes_ref, signs_ref, merge_ref, basis_ref, scores_ref,
    held, signs, merge, turned, given, pairs, far, mixed, stacks, low_maps, up_maps, outer, x_ref,
    flats, parts, wide, products, projected, gram_part, gram_recv, gram, low_part, low_recv, low_gram,
    up_part, up_recv, up_gram, up_other, score_part, hop_recv, score_recv,
    loaded, small, give_send, give_got, far_send, far_got, core_send, core_got,
    cross_send, cross_got, gram_send, gram_got, gram_send2, gram_got2,
    hop_send, hop_got, score_send, score_got,
    low_send, low_got, low_send2, low_got2, up_send, up_got, up_send2, up_got2, map_send, map_got,
):
    coord = lax.axis_index("coord")
    cohort = lax.axis_index("cohort")
    side = lax.rem(cohort, 2)
    upper = lax.rem(cohort // 2, 2)
    base = cohort - side
    partner = {"cohort": cohort + 1 - 2 * side}
    across = {"cohort": cohort + 2 - 4 * upper}
    corner = {"cohort": cohort + 2 - 4 * upper + 1 - 2 * side}
    line = (coord, n, lambda r: {"coord": r})
    pair = (
        coord * 2 + side, 2 * n, lambda r: {"coord": r // 2, "cohort": base + lax.rem(r, 2)}
    )
    chunks = held.shape[0] // 2
    early = chunks // 2
    piece = tile // 2
    raw = far.shape[1]
    width = turned.shape[0]

    def rows_of(c):
        return pl.ds(pl.multiple_of(c * tile, tile), tile)

    def piece_of(which, p):
        at = turn_of(which, p // 2) * tile + (p % 2) * piece
        return pl.ds(pl.multiple_of(at, piece), piece)

    def turn_of(which, i):
        return lax.rem(i + which * early, chunks)

    small_copies = [
        pltpu.make_async_copy(signs_ref, signs, small.at[0]),
        pltpu.make_async_copy(merge_ref, merge, small.at[1]),
    ]
    start(small_copies)

    def load(j):
        h = side if j % 2 else 1 - side
        at = pl.multiple_of((h * chunks + turn_of(upper, j // 2)) * tile, tile)
        return pltpu.make_async_copy(shapes_ref.at[:, pl.ds(at, tile)], held.at[j], loaded.at[j])

    for j in range(3):
        load(j).start()

    barrier = pltpu.get_barrier_semaphore()
    me, size, ident = pair
    for d in range(1, size):
        pl.semaphore_signal(
            barrier, inc=1, device_id=ident(lax.rem(me + d, size)), device_id_type=MESH
        )
    pl.semaphore_signal(barrier, inc=1, device_id=across, device_id_type=MESH)
    pl.semaphore_signal(barrier, inc=1, device_id=corner, device_id_type=MESH)
    wide[...] = jnp.zeros_like(wide)
    products[...] = jnp.zeros_like(products)

    def give(c):
        return remote(
            given.at[rows_of(c)], pairs.at[side, rows_of(c)], give_send.at[c], give_got.at[c], partner
        )

    def far_given(p):
        return remote(
            given.at[piece_of(upper, p)], far.at[side, p], far_send.at[0, p], far_got.at[0, p], corner
        )

    def far_mine(p):
        return remote(
            pairs.at[side, piece_of(upper, p)], far.at[side, p],
            far_send.at[1, p], far_got.at[1, p], across,
        )

    def center(j):
        load(j).wait()
        if j + 3 < 2 * chunks:
            load(j + 3).start()
        block = held.at[j]
        mean = jnp.sum(block[...].astype(F32), axis=0, keepdims=True) * (1.0 / block.shape[0])
        block[...] = (block[...].astype(F32) - mean).astype(BF16)

    def sketch(j):
        flat = dot(turned[...], held[j])
        rows = flat.T
        if j % 2:
            pairs[side, rows_of(turn_of(upper, j // 2))] = rows
        else:
            given[rows_of(turn_of(upper, j // 2))] = rows
        high, mid = split(rows)
        flats[j % 2] = flat.astype(BF16)
        parts[j % 2, :, :width] = high
        parts[j % 2, :, width:] = mid

    def send_sketch(j):
        i = j // 2
        for p in range(2 * i, min(2 * i + 2, raw)):
            (far_mine(p) if j % 2 else far_given(p)).start()
        if j % 2 == 0:
            give(turn_of(upper, i)).start()

    center(0)
    small_copies[0].wait()
    turned[...] = signs[...].astype(F32).T.astype(BF16)
    for j in range(2 * chunks):
        if j + 1 < 2 * chunks:
            center(j + 1)
        sketch(j)
        if j:
            wide[...] += dot(flats[(j - 1) % 2], parts[(j - 1) % 2])
        else:
            pl.semaphore_wait(barrier, size + 1)
        send_sketch(j)
    wide[...] += dot(flats[1], parts[1])
    turn = wide[:, width:]
    own = wide[:, :width] + turn + turn.T
    gram_part[...] = own.reshape(gram_part.shape)
    copies = scatter(gram_part, gram_recv, line, gram_send, gram_got)
    start(copies)

    def cross(i, carry):
        c = turn_of(upper, i)
        give(c).wait_recv()
        products[...] += cross_product(pairs[0, rows_of(c)], pairs[1, rows_of(c)])
        return carry

    lax.fori_loop(0, chunks, cross, 0)
    low_part[...] = products[...].reshape(low_part.shape)
    gram[coord] = summed(gram_part, gram_recv, line, copies)
    gathered = spread(gram, line, gram_send2, gram_got2)
    start(gathered)
    low_copies = scatter(low_part, low_recv, pair, low_send, low_got)
    start(low_copies)
    small_copies[1].wait()
    for l in range(2):
        outer[l] = dot_high(merge[l, 0], merge[l, 0], ((0,), (0,))) + dot_high(
            merge[l, 1], merge[l, 1], ((0,), (0,))
        )
    received(gathered)

    inverse_of(gram[...].reshape(width, width), x_ref)
    low_maps[upper, side] = dot_high(x_ref[...], merge[0, side], ((0,), (0,)))
    own_map = low_maps.at[upper, side]
    map_copies = [
        remote(own_map, own_map, map_send.at[i], map_got.at[i], device)
        for i, device in enumerate((partner, across, corner))
    ]
    start(map_copies)
    low_gram[pair[0]] = summed(low_part, low_recv, pair, low_copies)
    low_gathered = spread(low_gram, pair, low_send2, low_got2)
    start(low_gathered)
    map_copies[0].wait_recv()
    for i in range(2):
        stack_map(stacks.at[0], i, low_maps[upper, i])

    def ship(which, p):
        rows = mixed.at[which, side, piece_of(which, p)]
        return remote(rows, rows, cross_send.at[p], cross_got.at[p], across)

    def share(which, c):
        far_side = lax.rem(which + upper, 2)
        rows = mixed.at[far_side, side, rows_of(c)]
        return remote(rows, rows, core_send.at[which, c], core_got.at[which, c], partner)

    def blend(i):
        c = turn_of(upper, i)
        mixed[upper, side, rows_of(c)] = mix_rows(
            pairs[0, rows_of(c)], pairs[1, rows_of(c)], stacks.at[0]
        )
        share(0, c).start()
        return c

    for i in list(range(raw // 2, chunks)) + list(range(raw // 2)):
        blend(i)
        for p in range(max(2 * i, raw), 2 * i + 2):
            ship(upper, p).start()
    received(map_copies[1:])
    for i in range(2):
        stack_map(stacks.at[1], i, low_maps[1 - upper, i])

    products[...] = jnp.zeros_like(products)

    for p in range(2 * early):
        c = turn_of(1 - upper, p // 2)
        rows = piece_of(1 - upper, p)
        if p < raw:
            far_given(p).wait_recv()
            far_mine(p).wait_recv()
            mixed[1 - upper, side, rows] = mix_rows(far[0, p], far[1, p], stacks.at[1])
        else:
            ship(1 - upper, p).wait_recv()
        if p % 2:
            share(1, c).start()
        products[...] += cross_product(mixed[0, side, rows], mixed[1, side, rows])
    up_part[...] = products[...].reshape(up_part.shape)
    up_copies = scatter(up_part, up_recv, pair, up_send, up_got)
    start(up_copies)
    received(low_gathered)
    inner = dot_high(
        low_maps[upper, 0],
        dot_high(low_gram[...].reshape(width, width), low_maps[upper, 1], ((1,), (0,))),
        ((0,), (0,)),
    )
    inverse_of(outer[0] + inner + inner.T, x_ref)
    up_maps[upper] = dot_high(x_ref[...], merge[1, upper], ((0,), (0,)))
    up_other[upper] = summed(up_part, up_recv, pair, up_copies)
    up_swap = remote(up_other.at[upper], up_other.at[upper], map_send.at[3], map_got.at[3], across)
    up_swap.start()
    across_swap = remote(
        up_maps.at[upper], up_maps.at[upper], map_send.at[4], map_got.at[4], across
    )
    across_swap.start()

    projected[...] = jnp.zeros_like(projected)

    def project(h, i):
        c = turn_of(1 - upper, i)
        rows = jnp.concatenate(
            [mixed[0, h, rows_of(c)].astype(BF16), mixed[1, h, rows_of(c)].astype(BF16)], axis=1
        )
        place = 2 * lax.rem(i + early, chunks) + lax.rem(h + side + 1, 2)
        projected[...] += dot(held[place], rows)

    def project_given(i):
        c = turn_of(1 - upper, i)
        share(0, c).wait_recv()
        share(1, c).wait_recv()
        project(1 - side, i)

    def project_early(i, carry):
        project(side, i)
        project_given(i)
        return carry

    lax.fori_loop(0, early, project_early, 0)
    up_gathered = spread(up_gram, pair, up_send2, up_got2)
    for i in range(early, chunks):
        for p in range(2 * i, 2 * i + 2):
            ship(1 - upper, p).wait_recv()
        share(1, turn_of(1 - upper, i)).start()
        if i == chunks - 1:
            up_swap.wait_recv()
            up_gram[pair[0]] = up_other[0] + up_other[1]
            start(up_gathered)
        project(side, i)
    across_swap.wait_recv()
    for i in range(2):
        stack_map(stacks.at[0], i, up_maps[i])
    for i in range(early, chunks):
        project_given(i)

    block = score_part.shape[1]
    groups = n // 2
    group = coord // 2
    bit = lax.rem(coord, 2)

    def score_block(place):
        rows = projected[pl.ds(pl.multiple_of(place * block, block), block), :]
        score_part[place] = mix_rows(rows[:, :width], rows[:, width:], stacks.at[0])

    def hop(d):
        place = 2 * lax.rem(group + d, groups) + 1 - bit
        return remote(
            score_part.at[place], hop_recv.at[d], hop_send.at[d], hop_got.at[d],
            {"coord": coord + 1 - 2 * bit},
        )

    def relay(d):
        place = 2 * lax.rem(group + d, groups) + bit
        return remote(
            score_part.at[place], score_recv.at[d], score_send.at[d], score_got.at[d],
            {"coord": place},
        )

    order = list(range(1, groups)) + [0]
    for d in order:
        score_block(2 * lax.rem(group + d, groups) + 1 - bit)
        hop(d).start()
    for d in order:
        score_block(2 * lax.rem(group + d, groups) + bit)

    def between(t, tiles):
        for d in range(1, groups):
            if t == (tiles - 4) * d // (groups - 1):
                hop(d).wait_recv()
                place = 2 * lax.rem(group + d, groups) + bit
                score_part[place] = score_part[place] + hop_recv[d]
                relay(d).start()

    received(up_gathered)
    inner = dot_high(
        up_maps[0],
        dot_high(up_gram[...].reshape(width, width), up_maps[1], ((1,), (0,))),
        ((0,), (0,)),
    )
    inverse_of(outer[1] + inner + inner.T, x_ref, between)
    for i in range(2):
        stack_map(stacks.at[1], i, dot_high(up_maps[i], x_ref[...], ((1,), (1,))) * grow)

    def finish(c, carry):
        for h in range(2):
            basis_ref[h, rows_of(c)] = mix_rows(
                mixed[0, h, rows_of(c)], mixed[1, h, rows_of(c)], stacks.at[1]
            )
        return carry

    lax.fori_loop(0, chunks, finish, 0)
    hop(0).wait_recv()
    total = score_part[coord] + hop_recv[0]
    for d in range(1, groups):
        relay(d).wait_recv()
        total = total + score_recv[d]
    scores_ref[...] = dot_high(total, x_ref[...], ((1,), (1,))) * scale

    sent(copies + gathered + low_copies + low_gathered + up_copies + up_gathered)
    sent(map_copies + [across_swap, up_swap])
    for d in range(groups):
        hop(d).wait_send()
        if d:
            relay(d).wait_send()
    for p in range(2 * chunks):
        if p < raw:
            far_given(p).wait_send()
            far_mine(p).wait_send()
        else:
            ship(upper, p).wait_send()
    for c in range(chunks):
        give(c).wait_send()
        share(0, c).wait_send()
        share(1, c).wait_send()


def store_kernel(basis_ref, scores_ref, basis_out, scores_out, sems):
    copies = [
        pltpu.make_async_copy(basis_ref.at[h], basis_out.at[h], sems.at[h]) for h in range(2)
    ]
    copies.append(pltpu.make_async_copy(scores_ref, scores_out, sems.at[2]))
    start(copies)
    for copy in copies:
        copy.wait()


def on_device(shapes, sketch_signs, merge_sketch):
    n = lax.axis_size("coord")
    _, subjects, coords = shapes.shape
    width = sketch_signs.shape[2]
    half = coords // 2
    tile = math.gcd(half // 2, 512)
    chunks = half // tile
    raw = chunks
    rows = subjects // n
    line = (n, width // n, width)
    pair = (2 * n, width // (2 * n), width)
    scale = 4.0 * math.sqrt(width / (coords * n))
    grow = math.sqrt(coords * n)
    vmem, dma = pltpu.VMEM, pltpu.SemaphoreType.DMA
    basis, scores = pl.pallas_call(
        functools.partial(whole_kernel, n, tile, scale, grow),
        out_shape=(
            jax.ShapeDtypeStruct((2, half, width), F32),
            jax.ShapeDtypeStruct((rows, width), F32),
        ),
        in_specs=[pl.BlockSpec(memory_space=pltpu.HBM)] * 3,
        out_specs=(pl.BlockSpec(memory_space=vmem), pl.BlockSpec(memory_space=vmem)),
        scratch_shapes=[
            vmem((2 * chunks, subjects, tile), BF16),
            vmem((subjects, width), jnp.int32),
            vmem(merge_sketch.shape, F32),
            vmem((width, subjects), BF16),
            vmem((half, width), F32),
            vmem((2, half, width), F32),
            vmem((2, raw, tile // 2, width), F32),
            vmem((2, 2, half, width), F32),
            vmem((2, 6 * width, width), BF16),
            vmem((2, 2, width, width), F32),
            vmem((2, width, width), F32),
            vmem((2, width, width), F32),
            vmem((width, width), F32),
            vmem((2, width, tile), BF16),
            vmem((2, tile, 2 * width), BF16),
            vmem((width, 2 * width), F32),
            vmem((width, width), F32),
            vmem((subjects, 2 * width), F32),
        ]
        + [vmem(line, F32)] * 3
        + [vmem(pair, F32)] * 6
        + [
            vmem((2,) + pair[1:], F32),
            vmem((n, rows, width), F32),
            vmem((n // 2, rows, width), F32),
            vmem((n // 2, rows, width), F32),
            dma((2 * chunks,)),
            dma((2,)),
        ]
        + [dma((chunks,))] * 2
        + [dma((2, raw))] * 2
        + [dma((2, chunks))] * 2
        + [dma((2 * chunks,))] * 2
        + [dma((n,))] * 4
        + [dma((n // 2,))] * 4
        + [dma((2 * n,))] * 8
        + [dma((5,))] * 2,
        compiler_params=pltpu.CompilerParams(
            collective_id=0, has_side_effects=True, vmem_limit_bytes=48 * 1024 * 1024
        ),
        name="shape_pca",
    )(
        shapes[0],
        pltpu.with_memory_space_constraint(sketch_signs[0], pltpu.HBM),
        pltpu.with_memory_space_constraint(merge_sketch, pltpu.HBM),
    )
    basis, scores = pl.pallas_call(
        store_kernel,
        out_shape=(
            jax.ShapeDtypeStruct(basis.shape, F32),
            jax.ShapeDtypeStruct(scores.shape, F32),
        ),
        in_specs=[pl.BlockSpec(memory_space=vmem)] * 2,
        out_specs=(pl.BlockSpec(memory_space=pltpu.HBM),) * 2,
        scratch_shapes=[dma((3,))],
        name="store",
    )(
        pltpu.with_memory_space_constraint(basis, pltpu.VMEM),
        pltpu.with_memory_space_constraint(scores, pltpu.VMEM),
    )
    return basis.reshape(1, coords, width), scores[None]


def solution(mesh):
    placed = (P("cohort", None, "coord"), P("cohort", None, None), P())
    return jax.shard_map(
        on_device,
        mesh=mesh,
        in_specs=placed,
        out_specs=(P("cohort", "coord", None), P("cohort", "coord", None)),
        check_vma=False,
    )
```

```python
import functools
import math

import jax
import jax.numpy as jnp
from jax import lax
from jax.experimental import pallas as pl
from jax.experimental.pallas import tpu as pltpu
from jax.sharding import PartitionSpec as P

HIGHEST = lax.Precision.HIGHEST
MESH = pl.DeviceIdType.MESH
F32 = jnp.float32
BF16 = jnp.bfloat16


def dot(a, b):
    return jnp.dot(a, b, preferred_element_type=F32)


def dot_high(a, b, dims):
    return lax.dot_general(a, b, (dims, ((), ())), precision=HIGHEST, preferred_element_type=F32)


def split(x):
    high = x.astype(BF16)
    return high, (x - high.astype(F32)).astype(BF16)


def cross_product(a, b):
    dims = (((0,), (0,)), ((), ()))
    a_high, a_mid = split(a)
    b_high, b_mid = split(b)
    wide = lax.dot_general(
        a_high, jnp.concatenate([b_high, b_mid], axis=1), dims, preferred_element_type=F32
    )
    width = b.shape[1]
    return (
        wide[:, :width]
        + wide[:, width:]
        + lax.dot_general(a_mid, b_high, dims, preferred_element_type=F32)
    )


def stack_map(stacked, which, value):
    high, mid = split(value)
    width = value.shape[0]
    base = 3 * width * which
    stacked[base : base + width, :] = high
    stacked[base + width : base + 2 * width, :] = high
    stacked[base + 2 * width : base + 3 * width, :] = mid


def mix_rows(low, up, stacked):
    low_high, low_mid = split(low)
    up_high, up_mid = split(up)
    rows = jnp.concatenate([low_high, low_mid, low_high, up_high, up_mid, up_high], axis=1)
    return dot(rows, stacked[...])


def inverse_of(gram, x_ref, between=None):
    size = gram.shape[1]
    step = 8
    tiles = size // step
    lane = lax.broadcasted_iota(jnp.int32, (step, size), 1)
    sub = lax.broadcasted_iota(jnp.int32, (step, size), 0)

    def full(x):
        return jnp.broadcast_to(x, (step, size))

    def total(terms):
        while len(terms) > 1:
            terms = [terms[i] + terms[i + 1] for i in range(0, len(terms), 2)]
        return terms[0]

    both = [gram[t * step : (t + 1) * step, :] for t in range(tiles)]
    for t in range(tiles):
        at = t * step
        inside = (lane >= at) & (lane < at + step)
        cols = [full(both[t][:, at + k : at + k + 1]) for k in range(step)]
        e = [[full(cols[k][i : i + 1, :]) for k in range(i + 1)] for i in range(step)]
        head = jnp.where(inside, (lane - at == sub).astype(F32), both[t])
        rows = [full(head[i : i + 1, :]) for i in range(step)]
        f = {}
        inv = []
        for s in range(step):
            inv.append(1.0 / e[s][s])
            for i in range(s + 1, step):
                f[i, s] = e[i][s] * inv[s]
                for k in range(s + 1, i + 1):
                    e[i][k] = e[i][k] - f[i, s] * e[k][s]
            for i in range(s + 1, step):
                rows[i] = rows[i] - f[i, s] * rows[s]
        out = rows[0] * lax.rsqrt(e[0][0])
        for s in range(1, step):
            out = jnp.where(sub == s, rows[s] * lax.rsqrt(e[s][s]), out)
        x_ref[at : at + step, :] = jnp.where(lane < at + step, out, 0.0)
        rows = [rows[s] * inv[s] for s in range(step)]
        for u in range(t + 1, tiles):
            c = [full(both[u][:, at + s : at + s + 1]) for s in range(step)]
            for s in range(step):
                for r in range(s):
                    c[s] = c[s] - f[s, r] * c[r]
            both[u] = jnp.where(inside, 0.0, both[u]) - total([c[s] * rows[s] for s in range(step)])
        if between is not None:
            between(t, tiles)


def remote(src, dst, send, got, device):
    return pltpu.make_async_remote_copy(
        src_ref=src, dst_ref=dst, send_sem=send, recv_sem=got, device_id=device, device_id_type=MESH
    )


def scatter(part, recv, group, send, got):
    me, size, ident = group
    copies = []
    for d in range(1, size):
        peer = lax.rem(me + d, size)
        copies.append(remote(part.at[peer], recv.at[d], send.at[d], got.at[d], ident(peer)))
    return copies


def start(copies):
    for copy in copies:
        copy.start()


def summed(part, recv, group, copies):
    me, size, ident = group
    total = part[me]
    for d in range(1, size):
        copies[d - 1].wait_recv()
        total = total + recv[d]
    return total


def spread(out, group, send, got):
    me, size, ident = group
    return [
        remote(out.at[me], out.at[me], send.at[d], got.at[d], ident(lax.rem(me + d, size)))
        for d in range(1, size)
    ]


def received(copies):
    for copy in copies:
        copy.wait_recv()


def sent(copies):
    for copy in copies:
        copy.wait_send()


def whole_kernel(
    n, tile, scale, grow, shapes_ref, signs_ref, merge_ref, basis_ref, scores_ref,
    held, signs, merge, turned, given, pairs, far, mixed, stacks, low_maps, up_maps, outer, x_ref,
    flats, parts, wide, products, projected, gram_part, gram_recv, gram, low_part, low_recv, low_gram,
    up_part, up_recv, up_gram, up_sides, score_part, hop_recv, score_recv,
    loaded, small, give_send, give_got, far_send, far_got, core_send, core_got,
    cross_send, cross_got, gram_send, gram_got, gram_send2, gram_got2,
    hop_send, hop_got, score_send, score_got,
    low_send, low_got, low_send2, low_got2, up_send, up_got, up_send2, up_got2, map_send, map_got,
):
    coord = lax.axis_index("coord")
    cohort = lax.axis_index("cohort")
    side = lax.rem(cohort, 2)
    upper = lax.rem(cohort // 2, 2)
    base = cohort - side
    partner = {"cohort": cohort + 1 - 2 * side}
    across = {"cohort": cohort + 2 - 4 * upper}
    corner = {"cohort": cohort + 2 - 4 * upper + 1 - 2 * side}
    line = (coord, n, lambda r: {"coord": r})
    pair = (
        coord * 2 + side, 2 * n, lambda r: {"coord": r // 2, "cohort": base + lax.rem(r, 2)}
    )
    chunks = held.shape[0] // 2
    early = chunks // 2
    piece = tile // 2
    raw = far.shape[1]
    width = turned.shape[0]

    def rows_of(c):
        return pl.ds(pl.multiple_of(c * tile, tile), tile)

    def piece_of(which, p):
        at = turn_of(which, p // 2) * tile + (p % 2) * piece
        return pl.ds(pl.multiple_of(at, piece), piece)

    def turn_of(which, i):
        return lax.rem(i + which * early, chunks)

    small_copies = [
        pltpu.make_async_copy(signs_ref, signs, small.at[0]),
        pltpu.make_async_copy(merge_ref, merge, small.at[1]),
    ]
    start(small_copies)

    def load(j):
        h = side if j % 2 else 1 - side
        at = pl.multiple_of((h * chunks + turn_of(upper, j // 2)) * tile, tile)
        return pltpu.make_async_copy(shapes_ref.at[:, pl.ds(at, tile)], held.at[j], loaded.at[j])

    for j in range(3):
        load(j).start()

    barrier = pltpu.get_barrier_semaphore()
    me, size, ident = pair
    for d in range(1, size):
        pl.semaphore_signal(
            barrier, inc=1, device_id=ident(lax.rem(me + d, size)), device_id_type=MESH
        )
    pl.semaphore_signal(barrier, inc=1, device_id=across, device_id_type=MESH)
    pl.semaphore_signal(barrier, inc=1, device_id=corner, device_id_type=MESH)
    wide[...] = jnp.zeros_like(wide)
    products[...] = jnp.zeros_like(products)

    def give(c):
        return remote(
            given.at[rows_of(c)], pairs.at[side, rows_of(c)], give_send.at[c], give_got.at[c], partner
        )

    def far_given(p):
        return remote(
            given.at[piece_of(upper, p)], far.at[side, p], far_send.at[0, p], far_got.at[0, p], corner
        )

    def far_mine(p):
        return remote(
            pairs.at[side, piece_of(upper, p)], far.at[side, p],
            far_send.at[1, p], far_got.at[1, p], across,
        )

    def center(j):
        load(j).wait()
        if j + 3 < 2 * chunks:
            load(j + 3).start()
        block = held.at[j]
        mean = jnp.sum(block[...].astype(F32), axis=0, keepdims=True) * (1.0 / block.shape[0])
        block[...] = (block[...].astype(F32) - mean).astype(BF16)

    def sketch(j):
        flat = dot(turned[...], held[j])
        rows = flat.T
        if j % 2:
            pairs[side, rows_of(turn_of(upper, j // 2))] = rows
        else:
            given[rows_of(turn_of(upper, j // 2))] = rows
        high, mid = split(rows)
        flats[j % 2] = flat.astype(BF16)
        parts[j % 2, :, :width] = high
        parts[j % 2, :, width:] = mid

    def send_sketch(j):
        i = j // 2
        for p in range(2 * i, min(2 * i + 2, raw)):
            (far_mine(p) if j % 2 else far_given(p)).start()
        if j % 2 == 0:
            give(turn_of(upper, i)).start()

    center(0)
    small_copies[0].wait()
    turned[...] = signs[...].astype(F32).T.astype(BF16)
    for j in range(2 * chunks):
        if j + 1 < 2 * chunks:
            center(j + 1)
        sketch(j)
        if j:
            wide[...] += dot(flats[(j - 1) % 2], parts[(j - 1) % 2])
        else:
            pl.semaphore_wait(barrier, size + 1)
        send_sketch(j)
    wide[...] += dot(flats[1], parts[1])
    turn = wide[:, width:]
    own = wide[:, :width] + turn + turn.T
    gram_part[...] = own.reshape(gram_part.shape)
    copies = scatter(gram_part, gram_recv, line, gram_send, gram_got)
    start(copies)

    def cross(i, carry):
        c = turn_of(upper, i)
        give(c).wait_recv()
        products[...] += cross_product(pairs[0, rows_of(c)], pairs[1, rows_of(c)])
        return carry

    lax.fori_loop(0, chunks, cross, 0)
    low_part[...] = products[...].reshape(low_part.shape)
    gram[coord] = summed(gram_part, gram_recv, line, copies)
    gathered = spread(gram, line, gram_send2, gram_got2)
    start(gathered)
    low_copies = scatter(low_part, low_recv, pair, low_send, low_got)
    start(low_copies)
    small_copies[1].wait()
    for l in range(2):
        outer[l] = dot_high(merge[l, 0], merge[l, 0], ((0,), (0,))) + dot_high(
            merge[l, 1], merge[l, 1], ((0,), (0,))
        )
    received(gathered)

    inverse_of(gram[...].reshape(width, width), x_ref)
    low_maps[upper, side] = dot_high(x_ref[...], merge[0, side], ((0,), (0,)))
    own_map = low_maps.at[upper, side]
    map_copies = [
        remote(own_map, own_map, map_send.at[i], map_got.at[i], device)
        for i, device in enumerate((partner, across, corner))
    ]
    start(map_copies)
    low_gram[pair[0]] = summed(low_part, low_recv, pair, low_copies)
    low_gathered = spread(low_gram, pair, low_send2, low_got2)
    start(low_gathered)
    map_copies[0].wait_recv()
    for i in range(2):
        stack_map(stacks.at[0], i, low_maps[upper, i])

    def ship(which, p):
        rows = mixed.at[which, side, piece_of(which, p)]
        return remote(rows, rows, cross_send.at[p], cross_got.at[p], across)

    def share(which, c):
        far_side = lax.rem(which + upper, 2)
        rows = mixed.at[far_side, side, rows_of(c)]
        return remote(rows, rows, core_send.at[which, c], core_got.at[which, c], partner)

    def blend(i):
        c = turn_of(upper, i)
        mixed[upper, side, rows_of(c)] = mix_rows(
            pairs[0, rows_of(c)], pairs[1, rows_of(c)], stacks.at[0]
        )
        share(0, c).start()
        return c

    for i in list(range(raw // 2, chunks)) + list(range(raw // 2)):
        blend(i)
        for p in range(max(2 * i, raw), 2 * i + 2):
            ship(upper, p).start()
    received(map_copies[1:])
    for i in range(2):
        stack_map(stacks.at[1], i, low_maps[1 - upper, i])

    products[...] = jnp.zeros_like(products)

    for p in range(2 * early):
        c = turn_of(1 - upper, p // 2)
        rows = piece_of(1 - upper, p)
        if p < raw:
            far_given(p).wait_recv()
            far_mine(p).wait_recv()
            mixed[1 - upper, side, rows] = mix_rows(far[0, p], far[1, p], stacks.at[1])
        else:
            ship(1 - upper, p).wait_recv()
        if p % 2:
            share(1, c).start()
        products[...] += cross_product(mixed[0, side, rows], mixed[1, side, rows])
    up_part[...] = products[...].reshape(up_part.shape)
    up_copies = scatter(up_part, up_recv, pair, up_send, up_got)
    start(up_copies)
    received(low_gathered)
    inner = dot_high(
        low_maps[upper, 0],
        dot_high(low_gram[...].reshape(width, width), low_maps[upper, 1], ((1,), (0,))),
        ((0,), (0,)),
    )
    inverse_of(outer[0] + inner + inner.T, x_ref)
    up_maps[upper] = dot_high(x_ref[...], merge[1, upper], ((0,), (0,)))
    up_gram[pair[0]] = summed(up_part, up_recv, pair, up_copies)
    up_gathered = spread(up_gram, pair, up_send2, up_got2)
    start(up_gathered)
    across_swap = remote(
        up_maps.at[upper], up_maps.at[upper], map_send.at[4], map_got.at[4], across
    )
    across_swap.start()

    projected[...] = jnp.zeros_like(projected)

    def project(h, i):
        c = turn_of(1 - upper, i)
        rows = jnp.concatenate(
            [mixed[0, h, rows_of(c)].astype(BF16), mixed[1, h, rows_of(c)].astype(BF16)], axis=1
        )
        place = 2 * lax.rem(i + early, chunks) + lax.rem(h + side + 1, 2)
        projected[...] += dot(held[place], rows)

    def project_given(i):
        c = turn_of(1 - upper, i)
        share(0, c).wait_recv()
        share(1, c).wait_recv()
        project(1 - side, i)

    def project_early(i, carry):
        project(side, i)
        project_given(i)
        return carry

    lax.fori_loop(0, early, project_early, 0)
    received(up_gathered)
    up_sides[upper] = up_gram[...].reshape(width, width)
    up_swap = remote(up_sides.at[upper], up_sides.at[upper], map_send.at[3], map_got.at[3], across)
    up_swap.start()
    for i in range(early, chunks):
        for p in range(2 * i, 2 * i + 2):
            ship(1 - upper, p).wait_recv()
        share(1, turn_of(1 - upper, i)).start()
        project(side, i)
    across_swap.wait_recv()
    for i in range(2):
        stack_map(stacks.at[0], i, up_maps[i])
    for i in range(early, chunks):
        project_given(i)

    block = score_part.shape[1]
    groups = n // 2
    group = coord // 2
    bit = lax.rem(coord, 2)

    def score_block(place):
        rows = projected[pl.ds(pl.multiple_of(place * block, block), block), :]
        score_part[place] = mix_rows(rows[:, :width], rows[:, width:], stacks.at[0])

    def hop(d):
        place = 2 * lax.rem(group + d, groups) + 1 - bit
        return remote(
            score_part.at[place], hop_recv.at[d], hop_send.at[d], hop_got.at[d],
            {"coord": coord + 1 - 2 * bit},
        )

    def relay(d):
        place = 2 * lax.rem(group + d, groups) + bit
        return remote(
            score_part.at[place], score_recv.at[d], score_send.at[d], score_got.at[d],
            {"coord": place},
        )

    order = list(range(1, groups)) + [0]
    for d in order:
        score_block(2 * lax.rem(group + d, groups) + 1 - bit)
        hop(d).start()
    for d in order:
        score_block(2 * lax.rem(group + d, groups) + bit)

    def between(t, tiles):
        for d in range(1, groups):
            if t == (tiles - 4) * d // (groups - 1):
                hop(d).wait_recv()
                place = 2 * lax.rem(group + d, groups) + bit
                score_part[place] = score_part[place] + hop_recv[d]
                relay(d).start()

    up_swap.wait_recv()
    inner = dot_high(
        up_maps[0],
        dot_high(up_sides[0] + up_sides[1], up_maps[1], ((1,), (0,))),
        ((0,), (0,)),
    )
    inverse_of(outer[1] + inner + inner.T, x_ref, between)
    for i in range(2):
        stack_map(stacks.at[1], i, dot_high(up_maps[i], x_ref[...], ((1,), (1,))) * grow)

    def finish(c, carry):
        for h in range(2):
            basis_ref[h, rows_of(c)] = mix_rows(
                mixed[0, h, rows_of(c)], mixed[1, h, rows_of(c)], stacks.at[1]
            )
        return carry

    lax.fori_loop(0, chunks, finish, 0)
    hop(0).wait_recv()
    total = score_part[coord] + hop_recv[0]
    for d in range(1, groups):
        relay(d).wait_recv()
        total = total + score_recv[d]
    scores_ref[...] = dot_high(total, x_ref[...], ((1,), (1,))) * scale

    sent(copies + gathered + low_copies + low_gathered + up_copies + up_gathered)
    sent(map_copies + [across_swap, up_swap])
    for d in range(groups):
        hop(d).wait_send()
        if d:
            relay(d).wait_send()
    for p in range(2 * chunks):
        if p < raw:
            far_given(p).wait_send()
            far_mine(p).wait_send()
        else:
            ship(upper, p).wait_send()
    for c in range(chunks):
        give(c).wait_send()
        share(0, c).wait_send()
        share(1, c).wait_send()


def store_kernel(basis_ref, scores_ref, basis_out, scores_out, sems):
    copies = [
        pltpu.make_async_copy(basis_ref.at[h], basis_out.at[h], sems.at[h]) for h in range(2)
    ]
    copies.append(pltpu.make_async_copy(scores_ref, scores_out, sems.at[2]))
    start(copies)
    for copy in copies:
        copy.wait()


def on_device(shapes, sketch_signs, merge_sketch):
    n = lax.axis_size("coord")
    _, subjects, coords = shapes.shape
    width = sketch_signs.shape[2]
    half = coords // 2
    tile = math.gcd(half // 2, 512)
    chunks = half // tile
    raw = max(1, 3 * chunks // 4)
    rows = subjects // n
    line = (n, width // n, width)
    pair = (2 * n, width // (2 * n), width)
    scale = 4.0 * math.sqrt(width / (coords * n))
    grow = math.sqrt(coords * n)
    vmem, dma = pltpu.VMEM, pltpu.SemaphoreType.DMA
    basis, scores = pl.pallas_call(
        functools.partial(whole_kernel, n, tile, scale, grow),
        out_shape=(
            jax.ShapeDtypeStruct((2, half, width), F32),
            jax.ShapeDtypeStruct((rows, width), F32),
        ),
        in_specs=[pl.BlockSpec(memory_space=pltpu.HBM)] * 3,
        out_specs=(pl.BlockSpec(memory_space=vmem), pl.BlockSpec(memory_space=vmem)),
        scratch_shapes=[
            vmem((2 * chunks, subjects, tile), BF16),
            vmem((subjects, width), jnp.int32),
            vmem(merge_sketch.shape, F32),
            vmem((width, subjects), BF16),
            vmem((half, width), F32),
            vmem((2, half, width), F32),
            vmem((2, raw, tile // 2, width), F32),
            vmem((2, 2, half, width), F32),
            vmem((2, 6 * width, width), BF16),
            vmem((2, 2, width, width), F32),
            vmem((2, width, width), F32),
            vmem((2, width, width), F32),
            vmem((width, width), F32),
            vmem((2, width, tile), BF16),
            vmem((2, tile, 2 * width), BF16),
            vmem((width, 2 * width), F32),
            vmem((width, width), F32),
            vmem((subjects, 2 * width), F32),
        ]
        + [vmem(line, F32)] * 3
        + [vmem(pair, F32)] * 6
        + [
            vmem((2, width, width), F32),
            vmem((n, rows, width), F32),
            vmem((n // 2, rows, width), F32),
            vmem((n // 2, rows, width), F32),
            dma((2 * chunks,)),
            dma((2,)),
        ]
        + [dma((chunks,))] * 2
        + [dma((2, raw))] * 2
        + [dma((2, chunks))] * 2
        + [dma((2 * chunks,))] * 2
        + [dma((n,))] * 4
        + [dma((n // 2,))] * 4
        + [dma((2 * n,))] * 8
        + [dma((5,))] * 2,
        compiler_params=pltpu.CompilerParams(
            collective_id=0, has_side_effects=True, vmem_limit_bytes=48 * 1024 * 1024
        ),
        name="shape_pca",
    )(
        shapes[0],
        pltpu.with_memory_space_constraint(sketch_signs[0], pltpu.HBM),
        pltpu.with_memory_space_constraint(merge_sketch, pltpu.HBM),
    )
    basis, scores = pl.pallas_call(
        store_kernel,
        out_shape=(
            jax.ShapeDtypeStruct(basis.shape, F32),
            jax.ShapeDtypeStruct(scores.shape, F32),
        ),
        in_specs=[pl.BlockSpec(memory_space=vmem)] * 2,
        out_specs=(pl.BlockSpec(memory_space=pltpu.HBM),) * 2,
        scratch_shapes=[dma((3,))],
        name="store",
    )(
        pltpu.with_memory_space_constraint(basis, pltpu.VMEM),
        pltpu.with_memory_space_constraint(scores, pltpu.VMEM),
    )
    return basis.reshape(1, coords, width), scores[None]


def solution(mesh):
    placed = (P("cohort", None, "coord"), P("cohort", None, None), P())
    return jax.shard_map(
        on_device,
        mesh=mesh,
        in_specs=placed,
        out_specs=(P("cohort", "coord", None), P("cohort", "coord", None)),
        check_vma=False,
    )
```

```python
import functools
import math

import jax
import jax.numpy as jnp
from jax import lax
from jax.experimental import pallas as pl
from jax.experimental.pallas import tpu as pltpu
from jax.sharding import PartitionSpec as P

HIGHEST = lax.Precision.HIGHEST
MESH = pl.DeviceIdType.MESH
F32 = jnp.float32
BF16 = jnp.bfloat16


def dot(a, b):
    return jnp.dot(a, b, preferred_element_type=F32)


def dot_high(a, b, dims):
    return lax.dot_general(a, b, (dims, ((), ())), precision=HIGHEST, preferred_element_type=F32)


def split(x):
    high = x.astype(BF16)
    return high, (x - high.astype(F32)).astype(BF16)


def cross_product(a, b):
    dims = (((0,), (0,)), ((), ()))
    a_high, a_mid = split(a)
    b_high, b_mid = split(b)
    wide = lax.dot_general(
        a_high, jnp.concatenate([b_high, b_mid], axis=1), dims, preferred_element_type=F32
    )
    width = b.shape[1]
    return (
        wide[:, :width]
        + wide[:, width:]
        + lax.dot_general(a_mid, b_high, dims, preferred_element_type=F32)
    )


def stack_map(stacked, which, value):
    high, mid = split(value)
    width = value.shape[0]
    base = 3 * width * which
    stacked[base : base + width, :] = high
    stacked[base + width : base + 2 * width, :] = high
    stacked[base + 2 * width : base + 3 * width, :] = mid


def mix_rows(low, up, stacked):
    low_high, low_mid = split(low)
    up_high, up_mid = split(up)
    rows = jnp.concatenate([low_high, low_mid, low_high, up_high, up_mid, up_high], axis=1)
    return dot(rows, stacked[...])


def inverse_of(gram, x_ref, between=None):
    size = gram.shape[1]
    step = 8
    tiles = size // step
    lane = lax.broadcasted_iota(jnp.int32, (step, size), 1)
    sub = lax.broadcasted_iota(jnp.int32, (step, size), 0)

    def full(x):
        return jnp.broadcast_to(x, (step, size))

    def total(terms):
        while len(terms) > 1:
            terms = [terms[i] + terms[i + 1] for i in range(0, len(terms), 2)]
        return terms[0]

    both = [gram[t * step : (t + 1) * step, :] for t in range(tiles)]
    for t in range(tiles):
        at = t * step
        inside = (lane >= at) & (lane < at + step)
        cols = [full(both[t][:, at + k : at + k + 1]) for k in range(step)]
        e = [[full(cols[k][i : i + 1, :]) for k in range(i + 1)] for i in range(step)]
        head = jnp.where(inside, (lane - at == sub).astype(F32), both[t])
        rows = [full(head[i : i + 1, :]) for i in range(step)]
        f = {}
        inv = []
        for s in range(step):
            inv.append(1.0 / e[s][s])
            for i in range(s + 1, step):
                f[i, s] = e[i][s] * inv[s]
                for k in range(s + 1, i + 1):
                    e[i][k] = e[i][k] - f[i, s] * e[k][s]
            for i in range(s + 1, step):
                rows[i] = rows[i] - f[i, s] * rows[s]
        out = rows[0] * lax.rsqrt(e[0][0])
        for s in range(1, step):
            out = jnp.where(sub == s, rows[s] * lax.rsqrt(e[s][s]), out)
        x_ref[at : at + step, :] = jnp.where(lane < at + step, out, 0.0)
        rows = [rows[s] * inv[s] for s in range(step)]
        for u in range(t + 1, tiles):
            c = [full(both[u][:, at + s : at + s + 1]) for s in range(step)]
            for s in range(step):
                for r in range(s):
                    c[s] = c[s] - f[s, r] * c[r]
            both[u] = jnp.where(inside, 0.0, both[u]) - total([c[s] * rows[s] for s in range(step)])
        if between is not None:
            between(t, tiles)


def remote(src, dst, send, got, device):
    return pltpu.make_async_remote_copy(
        src_ref=src, dst_ref=dst, send_sem=send, recv_sem=got, device_id=device, device_id_type=MESH
    )


def scatter(part, recv, group, send, got):
    me, size, ident = group
    copies = []
    for d in range(1, size):
        peer = lax.rem(me + d, size)
        copies.append(remote(part.at[peer], recv.at[d], send.at[d], got.at[d], ident(peer)))
    return copies


def start(copies):
    for copy in copies:
        copy.start()


def summed(part, recv, group, copies):
    me, size, ident = group
    total = part[me]
    for d in range(1, size):
        copies[d - 1].wait_recv()
        total = total + recv[d]
    return total


def spread(out, group, send, got):
    me, size, ident = group
    return [
        remote(out.at[me], out.at[me], send.at[d], got.at[d], ident(lax.rem(me + d, size)))
        for d in range(1, size)
    ]


def received(copies):
    for copy in copies:
        copy.wait_recv()


def sent(copies):
    for copy in copies:
        copy.wait_send()


def whole_kernel(
    n, tile, scale, grow, shapes_ref, signs_ref, merge_ref, basis_ref, scores_ref,
    held, signs, merge, turned, given, pairs, far, mixed, stacks, low_maps, up_maps, outer, x_ref,
    flats, parts, wide, products, projected, gram_part, gram_recv, gram, low_part, low_recv, low_gram,
    up_part, up_recv, up_gram, up_sides, score_part, hop_recv, score_recv,
    loaded, small, give_send, give_got, far_send, far_got, core_send, core_got,
    cross_send, cross_got, gram_send, gram_got, gram_send2, gram_got2,
    hop_send, hop_got, score_send, score_got,
    low_send, low_got, low_send2, low_got2, up_send, up_got, up_send2, up_got2, map_send, map_got,
):
    coord = lax.axis_index("coord")
    cohort = lax.axis_index("cohort")
    side = lax.rem(cohort, 2)
    upper = lax.rem(cohort // 2, 2)
    base = cohort - side
    partner = {"cohort": cohort + 1 - 2 * side}
    across = {"cohort": cohort + 2 - 4 * upper}
    corner = {"cohort": cohort + 2 - 4 * upper + 1 - 2 * side}
    line = (coord, n, lambda r: {"coord": r})
    pair = (
        coord * 2 + side, 2 * n, lambda r: {"coord": r // 2, "cohort": base + lax.rem(r, 2)}
    )
    chunks = held.shape[0] // 2
    early = chunks // 2
    piece = tile // 2
    raw = far.shape[1]
    width = turned.shape[0]

    def rows_of(c):
        return pl.ds(pl.multiple_of(c * tile, tile), tile)

    def piece_of(which, p):
        at = turn_of(which, p // 2) * tile + (p % 2) * piece
        return pl.ds(pl.multiple_of(at, piece), piece)

    def turn_of(which, i):
        return lax.rem(i + which * early, chunks)

    small_copies = [
        pltpu.make_async_copy(signs_ref, signs, small.at[0]),
        pltpu.make_async_copy(merge_ref, merge, small.at[1]),
    ]
    start(small_copies)

    def load(j):
        h = side if j % 2 else 1 - side
        at = pl.multiple_of((h * chunks + turn_of(upper, j // 2)) * tile, tile)
        return pltpu.make_async_copy(shapes_ref.at[:, pl.ds(at, tile)], held.at[j], loaded.at[j])

    for j in range(3):
        load(j).start()

    barrier = pltpu.get_barrier_semaphore()
    me, size, ident = pair
    for d in range(1, size):
        pl.semaphore_signal(
            barrier, inc=1, device_id=ident(lax.rem(me + d, size)), device_id_type=MESH
        )
    pl.semaphore_signal(barrier, inc=1, device_id=across, device_id_type=MESH)
    pl.semaphore_signal(barrier, inc=1, device_id=corner, device_id_type=MESH)
    wide[...] = jnp.zeros_like(wide)
    products[...] = jnp.zeros_like(products)

    def give(c):
        return remote(
            given.at[rows_of(c)], pairs.at[side, rows_of(c)], give_send.at[c], give_got.at[c], partner
        )

    def far_given(p):
        return remote(
            given.at[piece_of(upper, p)], far.at[side, p], far_send.at[0, p], far_got.at[0, p], corner
        )

    def far_mine(p):
        return remote(
            pairs.at[side, piece_of(upper, p)], far.at[side, p],
            far_send.at[1, p], far_got.at[1, p], across,
        )

    def center(j):
        load(j).wait()
        if j + 3 < 2 * chunks:
            load(j + 3).start()
        block = held.at[j]
        mean = jnp.sum(block[...].astype(F32), axis=0, keepdims=True) * (1.0 / block.shape[0])
        block[...] = (block[...].astype(F32) - mean).astype(BF16)

    def sketch(j):
        flat = dot(turned[...], held[j])
        rows = flat.T
        if j % 2:
            pairs[side, rows_of(turn_of(upper, j // 2))] = rows
        else:
            given[rows_of(turn_of(upper, j // 2))] = rows
        high, mid = split(rows)
        flats[j % 2] = flat.astype(BF16)
        parts[j % 2, :, :width] = high
        parts[j % 2, :, width:] = mid

    def send_sketch(j):
        i = j // 2
        for p in range(2 * i, min(2 * i + 2, raw)):
            (far_mine(p) if j % 2 else far_given(p)).start()
        if j % 2 == 0:
            give(turn_of(upper, i)).start()

    center(0)
    small_copies[0].wait()
    turned[...] = signs[...].astype(F32).T.astype(BF16)
    for j in range(2 * chunks):
        if j + 1 < 2 * chunks:
            center(j + 1)
        sketch(j)
        if j:
            wide[...] += dot(flats[(j - 1) % 2], parts[(j - 1) % 2])
        else:
            pl.semaphore_wait(barrier, size + 1)
        send_sketch(j)
    wide[...] += dot(flats[1], parts[1])
    turn = wide[:, width:]
    own = wide[:, :width] + turn + turn.T
    gram_part[...] = own.reshape(gram_part.shape)
    copies = scatter(gram_part, gram_recv, line, gram_send, gram_got)
    start(copies)

    def cross(i, carry):
        c = turn_of(upper, i)
        give(c).wait_recv()
        products[...] += cross_product(pairs[0, rows_of(c)], pairs[1, rows_of(c)])
        return carry

    lax.fori_loop(0, chunks, cross, 0)
    low_part[...] = products[...].reshape(low_part.shape)
    gram[coord] = summed(gram_part, gram_recv, line, copies)
    gathered = spread(gram, line, gram_send2, gram_got2)
    start(gathered)
    low_copies = scatter(low_part, low_recv, pair, low_send, low_got)
    start(low_copies)
    small_copies[1].wait()
    for l in range(2):
        outer[l] = dot_high(merge[l, 0], merge[l, 0], ((0,), (0,))) + dot_high(
            merge[l, 1], merge[l, 1], ((0,), (0,))
        )
    received(gathered)

    inverse_of(gram[...].reshape(width, width), x_ref)
    low_maps[upper, side] = dot_high(x_ref[...], merge[0, side], ((0,), (0,)))
    own_map = low_maps.at[upper, side]
    map_copies = [
        remote(own_map, own_map, map_send.at[i], map_got.at[i], device)
        for i, device in enumerate((partner, across))
    ]
    start(map_copies)
    low_gram[pair[0]] = summed(low_part, low_recv, pair, low_copies)
    low_gathered = spread(low_gram, pair, low_send2, low_got2)
    start(low_gathered)
    map_copies[0].wait_recv()
    for i in range(2):
        stack_map(stacks.at[0], i, low_maps[upper, i])

    def ship(which, p):
        rows = mixed.at[which, side, piece_of(which, p)]
        return remote(rows, rows, cross_send.at[p], cross_got.at[p], across)

    def share(which, c):
        far_side = lax.rem(which + upper, 2)
        rows = mixed.at[far_side, side, rows_of(c)]
        return remote(rows, rows, core_send.at[which, c], core_got.at[which, c], partner)

    def blend(i):
        c = turn_of(upper, i)
        mixed[upper, side, rows_of(c)] = mix_rows(
            pairs[0, rows_of(c)], pairs[1, rows_of(c)], stacks.at[0]
        )
        share(0, c).start()
        return c

    for i in list(range(raw // 2, chunks)) + list(range(raw // 2)):
        blend(i)
        for p in range(max(2 * i, raw), 2 * i + 2):
            ship(upper, p).start()
    map_copies[1].wait_recv()
    far_map = low_maps.at[1 - upper, side]
    map_copies.append(remote(far_map, far_map, map_send.at[2], map_got.at[2], partner))
    map_copies[2].start()
    map_copies[2].wait_recv()
    for i in range(2):
        stack_map(stacks.at[1], i, low_maps[1 - upper, i])

    products[...] = jnp.zeros_like(products)

    for p in range(2 * early):
        c = turn_of(1 - upper, p // 2)
        rows = piece_of(1 - upper, p)
        if p < raw:
            far_given(p).wait_recv()
            far_mine(p).wait_recv()
            mixed[1 - upper, side, rows] = mix_rows(far[0, p], far[1, p], stacks.at[1])
        else:
            ship(1 - upper, p).wait_recv()
        if p % 2:
            share(1, c).start()
        products[...] += cross_product(mixed[0, side, rows], mixed[1, side, rows])
    up_part[...] = products[...].reshape(up_part.shape)
    up_copies = scatter(up_part, up_recv, pair, up_send, up_got)
    start(up_copies)
    received(low_gathered)
    inner = dot_high(
        low_maps[upper, 0],
        dot_high(low_gram[...].reshape(width, width), low_maps[upper, 1], ((1,), (0,))),
        ((0,), (0,)),
    )
    inverse_of(outer[0] + inner + inner.T, x_ref)
    up_maps[upper] = dot_high(x_ref[...], merge[1, upper], ((0,), (0,)))
    up_gram[pair[0]] = summed(up_part, up_recv, pair, up_copies)
    up_gathered = spread(up_gram, pair, up_send2, up_got2)
    start(up_gathered)
    across_swap = remote(
        up_maps.at[upper], up_maps.at[upper], map_send.at[4], map_got.at[4], across
    )
    across_swap.start()

    projected[...] = jnp.zeros_like(projected)

    def project(h, i):
        c = turn_of(1 - upper, i)
        rows = jnp.concatenate(
            [mixed[0, h, rows_of(c)].astype(BF16), mixed[1, h, rows_of(c)].astype(BF16)], axis=1
        )
        place = 2 * lax.rem(i + early, chunks) + lax.rem(h + side + 1, 2)
        projected[...] += dot(held[place], rows)

    def project_given(i):
        c = turn_of(1 - upper, i)
        share(0, c).wait_recv()
        share(1, c).wait_recv()
        project(1 - side, i)

    def project_early(i, carry):
        project(side, i)
        project_given(i)
        return carry

    lax.fori_loop(0, early, project_early, 0)
    received(up_gathered)
    up_sides[upper] = up_gram[...].reshape(width, width)
    up_swap = remote(up_sides.at[upper], up_sides.at[upper], map_send.at[3], map_got.at[3], across)
    up_swap.start()
    for i in range(early, chunks):
        for p in range(2 * i, 2 * i + 2):
            ship(1 - upper, p).wait_recv()
        share(1, turn_of(1 - upper, i)).start()
        project(side, i)
    across_swap.wait_recv()
    for i in range(2):
        stack_map(stacks.at[0], i, up_maps[i])
    for i in range(early, chunks):
        project_given(i)

    block = score_part.shape[1]
    groups = n // 2
    group = coord // 2
    bit = lax.rem(coord, 2)

    def score_pair(g):
        rows = projected[pl.ds(pl.multiple_of(2 * g * block, 2 * block), 2 * block), :]
        both = mix_rows(rows[:, :width], rows[:, width:], stacks.at[0])
        score_part[2 * g] = both[:block]
        score_part[2 * g + 1] = both[block:]

    def hop(d):
        place = 2 * lax.rem(group + d, groups) + 1 - bit
        return remote(
            score_part.at[place], hop_recv.at[d], hop_send.at[d], hop_got.at[d],
            {"coord": coord + 1 - 2 * bit},
        )

    def relay(d):
        place = 2 * lax.rem(group + d, groups) + bit
        return remote(
            score_part.at[place], score_recv.at[d], score_send.at[d], score_got.at[d],
            {"coord": place},
        )

    for d in list(range(1, groups)) + [0]:
        score_pair(lax.rem(group + d, groups))
        hop(d).start()

    def between(t, tiles):
        for d in range(1, groups):
            if t == (tiles - 4) * d // (groups - 1):
                hop(d).wait_recv()
                place = 2 * lax.rem(group + d, groups) + bit
                score_part[place] = score_part[place] + hop_recv[d]
                relay(d).start()

    up_swap.wait_recv()
    inner = dot_high(
        up_maps[0],
        dot_high(up_sides[0] + up_sides[1], up_maps[1], ((1,), (0,))),
        ((0,), (0,)),
    )
    inverse_of(outer[1] + inner + inner.T, x_ref, between)
    for i in range(2):
        stack_map(stacks.at[1], i, dot_high(up_maps[i], x_ref[...], ((1,), (1,))) * grow)

    def finish(c, carry):
        for h in range(2):
            basis_ref[h, rows_of(c)] = mix_rows(
                mixed[0, h, rows_of(c)], mixed[1, h, rows_of(c)], stacks.at[1]
            )
        return carry

    lax.fori_loop(0, chunks, finish, 0)
    hop(0).wait_recv()
    total = score_part[coord] + hop_recv[0]
    for d in range(1, groups):
        relay(d).wait_recv()
        total = total + score_recv[d]
    scores_ref[...] = dot_high(total, x_ref[...], ((1,), (1,))) * scale

    sent(copies + gathered + low_copies + low_gathered + up_copies + up_gathered)
    sent(map_copies + [across_swap, up_swap])
    for d in range(groups):
        hop(d).wait_send()
        if d:
            relay(d).wait_send()
    for p in range(2 * chunks):
        if p < raw:
            far_given(p).wait_send()
            far_mine(p).wait_send()
        else:
            ship(upper, p).wait_send()
    for c in range(chunks):
        give(c).wait_send()
        share(0, c).wait_send()
        share(1, c).wait_send()


def store_kernel(basis_ref, scores_ref, basis_out, scores_out, sems):
    copies = [
        pltpu.make_async_copy(basis_ref.at[h], basis_out.at[h], sems.at[h]) for h in range(2)
    ]
    copies.append(pltpu.make_async_copy(scores_ref, scores_out, sems.at[2]))
    start(copies)
    for copy in copies:
        copy.wait()


def on_device(shapes, sketch_signs, merge_sketch):
    n = lax.axis_size("coord")
    _, subjects, coords = shapes.shape
    width = sketch_signs.shape[2]
    half = coords // 2
    tile = math.gcd(half // 2, 512)
    chunks = half // tile
    raw = max(1, 3 * chunks // 4)
    rows = subjects // n
    line = (n, width // n, width)
    pair = (2 * n, width // (2 * n), width)
    scale = 4.0 * math.sqrt(width / (coords * n))
    grow = math.sqrt(coords * n)
    vmem, dma = pltpu.VMEM, pltpu.SemaphoreType.DMA
    basis, scores = pl.pallas_call(
        functools.partial(whole_kernel, n, tile, scale, grow),
        out_shape=(
            jax.ShapeDtypeStruct((2, half, width), F32),
            jax.ShapeDtypeStruct((rows, width), F32),
        ),
        in_specs=[pl.BlockSpec(memory_space=pltpu.HBM)] * 3,
        out_specs=(pl.BlockSpec(memory_space=vmem), pl.BlockSpec(memory_space=vmem)),
        scratch_shapes=[
            vmem((2 * chunks, subjects, tile), BF16),
            vmem((subjects, width), jnp.int32),
            vmem(merge_sketch.shape, F32),
            vmem((width, subjects), BF16),
            vmem((half, width), F32),
            vmem((2, half, width), F32),
            vmem((2, raw, tile // 2, width), F32),
            vmem((2, 2, half, width), F32),
            vmem((2, 6 * width, width), BF16),
            vmem((2, 2, width, width), F32),
            vmem((2, width, width), F32),
            vmem((2, width, width), F32),
            vmem((width, width), F32),
            vmem((2, width, tile), BF16),
            vmem((2, tile, 2 * width), BF16),
            vmem((width, 2 * width), F32),
            vmem((width, width), F32),
            vmem((subjects, 2 * width), F32),
        ]
        + [vmem(line, F32)] * 3
        + [vmem(pair, F32)] * 6
        + [
            vmem((2, width, width), F32),
            vmem((n, rows, width), F32),
            vmem((n // 2, rows, width), F32),
            vmem((n // 2, rows, width), F32),
            dma((2 * chunks,)),
            dma((2,)),
        ]
        + [dma((chunks,))] * 2
        + [dma((2, raw))] * 2
        + [dma((2, chunks))] * 2
        + [dma((2 * chunks,))] * 2
        + [dma((n,))] * 4
        + [dma((n // 2,))] * 4
        + [dma((2 * n,))] * 8
        + [dma((5,))] * 2,
        compiler_params=pltpu.CompilerParams(
            collective_id=0, has_side_effects=True, vmem_limit_bytes=48 * 1024 * 1024
        ),
        name="shape_pca",
    )(
        shapes[0],
        pltpu.with_memory_space_constraint(sketch_signs[0], pltpu.HBM),
        pltpu.with_memory_space_constraint(merge_sketch, pltpu.HBM),
    )
    basis, scores = pl.pallas_call(
        store_kernel,
        out_shape=(
            jax.ShapeDtypeStruct(basis.shape, F32),
            jax.ShapeDtypeStruct(scores.shape, F32),
        ),
        in_specs=[pl.BlockSpec(memory_space=vmem)] * 2,
        out_specs=(pl.BlockSpec(memory_space=pltpu.HBM),) * 2,
        scratch_shapes=[dma((3,))],
        name="store",
    )(
        pltpu.with_memory_space_constraint(basis, pltpu.VMEM),
        pltpu.with_memory_space_constraint(scores, pltpu.VMEM),
    )
    return basis.reshape(1, coords, width), scores[None]


def solution(mesh):
    placed = (P("cohort", None, "coord"), P("cohort", None, None), P())
    return jax.shard_map(
        on_device,
        mesh=mesh,
        in_specs=placed,
        out_specs=(P("cohort", "coord", None), P("cohort", "coord", None)),
        check_vma=False,
    )
```

```python
import functools
import math

import jax
import jax.numpy as jnp
from jax import lax
from jax.experimental import pallas as pl
from jax.experimental.pallas import tpu as pltpu
from jax.sharding import PartitionSpec as P

HIGHEST = lax.Precision.HIGHEST
MESH = pl.DeviceIdType.MESH
F32 = jnp.float32
BF16 = jnp.bfloat16


def dot(a, b):
    return jnp.dot(a, b, preferred_element_type=F32)


def dot_high(a, b, dims):
    return lax.dot_general(a, b, (dims, ((), ())), precision=HIGHEST, preferred_element_type=F32)


def split(x):
    high = x.astype(BF16)
    return high, (x - high.astype(F32)).astype(BF16)


def cross_product(a, b):
    dims = (((0,), (0,)), ((), ()))
    a_high, a_mid = split(a)
    b_high, b_mid = split(b)
    wide = lax.dot_general(
        a_high, jnp.concatenate([b_high, b_mid], axis=1), dims, preferred_element_type=F32
    )
    width = b.shape[1]
    return (
        wide[:, :width]
        + wide[:, width:]
        + lax.dot_general(a_mid, b_high, dims, preferred_element_type=F32)
    )


def stack_map(stacked, which, value):
    high, mid = split(value)
    width = value.shape[0]
    base = 3 * width * which
    stacked[base : base + width, :] = high
    stacked[base + width : base + 2 * width, :] = high
    stacked[base + 2 * width : base + 3 * width, :] = mid


def mix_rows(low, up, stacked):
    low_high, low_mid = split(low)
    up_high, up_mid = split(up)
    rows = jnp.concatenate([low_high, low_mid, low_high, up_high, up_mid, up_high], axis=1)
    return dot(rows, stacked[...])


def inverse_of(gram, x_ref, between=None):
    size = gram.shape[1]
    step = 8
    tiles = size // step
    lane = lax.broadcasted_iota(jnp.int32, (step, size), 1)
    sub = lax.broadcasted_iota(jnp.int32, (step, size), 0)

    def full(x):
        return jnp.broadcast_to(x, (step, size))

    def total(terms):
        while len(terms) > 1:
            terms = [terms[i] + terms[i + 1] for i in range(0, len(terms), 2)]
        return terms[0]

    both = [gram[t * step : (t + 1) * step, :] for t in range(tiles)]
    for t in range(tiles):
        at = t * step
        inside = (lane >= at) & (lane < at + step)
        cols = [full(both[t][:, at + k : at + k + 1]) for k in range(step)]
        e = [[full(cols[k][i : i + 1, :]) for k in range(i + 1)] for i in range(step)]
        head = jnp.where(inside, (lane - at == sub).astype(F32), both[t])
        rows = [full(head[i : i + 1, :]) for i in range(step)]
        f = {}
        inv = []
        for s in range(step):
            inv.append(1.0 / e[s][s])
            for i in range(s + 1, step):
                f[i, s] = e[i][s] * inv[s]
                for k in range(s + 1, i + 1):
                    e[i][k] = e[i][k] - f[i, s] * e[k][s]
            for i in range(s + 1, step):
                rows[i] = rows[i] - f[i, s] * rows[s]
        out = rows[0] * lax.rsqrt(e[0][0])
        for s in range(1, step):
            out = jnp.where(sub == s, rows[s] * lax.rsqrt(e[s][s]), out)
        x_ref[at : at + step, :] = jnp.where(lane < at + step, out, 0.0)
        rows = [rows[s] * inv[s] for s in range(step)]
        for u in range(t + 1, tiles):
            c = [full(both[u][:, at + s : at + s + 1]) for s in range(step)]
            for s in range(step):
                for r in range(s):
                    c[s] = c[s] - f[s, r] * c[r]
            both[u] = jnp.where(inside, 0.0, both[u]) - total([c[s] * rows[s] for s in range(step)])
        if between is not None:
            between(t, tiles)


def remote(src, dst, send, got, device):
    return pltpu.make_async_remote_copy(
        src_ref=src, dst_ref=dst, send_sem=send, recv_sem=got, device_id=device, device_id_type=MESH
    )


def scatter(part, recv, group, send, got):
    me, size, ident = group
    copies = []
    for d in range(1, size):
        peer = lax.rem(me + d, size)
        copies.append(remote(part.at[peer], recv.at[d], send.at[d], got.at[d], ident(peer)))
    return copies


def start(copies):
    for copy in copies:
        copy.start()


def summed(part, recv, group, copies):
    me, size, ident = group
    total = part[me]
    for d in range(1, size):
        copies[d - 1].wait_recv()
        total = total + recv[d]
    return total


def spread(out, group, send, got):
    me, size, ident = group
    return [
        remote(out.at[me], out.at[me], send.at[d], got.at[d], ident(lax.rem(me + d, size)))
        for d in range(1, size)
    ]


def received(copies):
    for copy in copies:
        copy.wait_recv()


def sent(copies):
    for copy in copies:
        copy.wait_send()


def whole_kernel(
    n, tile, scale, grow, shapes_ref, signs_ref, merge_ref, basis_ref, scores_ref,
    held, signs, merge, turned, given, pairs, far, mixed, stacks, low_maps, up_maps, outer, x_ref,
    flats, parts, wide, products, projected, gram_part, gram_recv, gram, low_part, low_recv, low_gram,
    up_part, up_recv, up_gram, up_sides, score_part, hop_recv, score_recv,
    loaded, small, give_send, give_got, far_send, far_got, core_send, core_got,
    cross_send, cross_got, gram_send, gram_got, gram_send2, gram_got2,
    hop_send, hop_got, score_send, score_got,
    low_send, low_got, low_send2, low_got2, up_send, up_got, up_send2, up_got2, map_send, map_got,
):
    coord = lax.axis_index("coord")
    cohort = lax.axis_index("cohort")
    side = lax.rem(cohort, 2)
    upper = lax.rem(cohort // 2, 2)
    base = cohort - side
    partner = {"cohort": cohort + 1 - 2 * side}
    across = {"cohort": cohort + 2 - 4 * upper}
    corner = {"cohort": cohort + 2 - 4 * upper + 1 - 2 * side}
    line = (coord, n, lambda r: {"coord": r})
    pair = (
        coord * 2 + side, 2 * n, lambda r: {"coord": r // 2, "cohort": base + lax.rem(r, 2)}
    )
    chunks = held.shape[0] // 2
    early = chunks // 2
    piece = tile // 2
    raw = far.shape[1]
    width = turned.shape[0]

    def rows_of(c):
        return pl.ds(pl.multiple_of(c * tile, tile), tile)

    def piece_of(which, p):
        at = turn_of(which, p // 2) * tile + (p % 2) * piece
        return pl.ds(pl.multiple_of(at, piece), piece)

    def turn_of(which, i):
        return lax.rem(i + which * early, chunks)

    small_copies = [
        pltpu.make_async_copy(signs_ref, signs, small.at[0]),
        pltpu.make_async_copy(merge_ref, merge, small.at[1]),
    ]
    small_copies[0].start()

    def load(j):
        h = side if j % 2 else 1 - side
        at = pl.multiple_of((h * chunks + turn_of(upper, j // 2)) * tile, tile)
        return pltpu.make_async_copy(shapes_ref.at[:, pl.ds(at, tile)], held.at[j], loaded.at[j])

    for j in range(3):
        load(j).start()
    small_copies[1].start()

    barrier = pltpu.get_barrier_semaphore()
    me, size, ident = pair
    for d in range(1, size):
        pl.semaphore_signal(
            barrier, inc=1, device_id=ident(lax.rem(me + d, size)), device_id_type=MESH
        )
    pl.semaphore_signal(barrier, inc=1, device_id=across, device_id_type=MESH)
    pl.semaphore_signal(barrier, inc=1, device_id=corner, device_id_type=MESH)
    wide[...] = jnp.zeros_like(wide)
    products[...] = jnp.zeros_like(products)

    def give(c):
        return remote(
            given.at[rows_of(c)], pairs.at[side, rows_of(c)], give_send.at[c], give_got.at[c], partner
        )

    def far_given(p):
        return remote(
            given.at[piece_of(upper, p)], far.at[side, p], far_send.at[0, p], far_got.at[0, p], corner
        )

    def far_mine(p):
        return remote(
            pairs.at[side, piece_of(upper, p)], far.at[side, p],
            far_send.at[1, p], far_got.at[1, p], across,
        )

    def center(j):
        load(j).wait()
        if j + 3 < 2 * chunks:
            load(j + 3).start()
        block = held.at[j]
        mean = jnp.sum(block[...].astype(F32), axis=0, keepdims=True) * (1.0 / block.shape[0])
        block[...] = (block[...].astype(F32) - mean).astype(BF16)

    def sketch(j):
        flat = dot(turned[...], held[j])
        rows = flat.T
        if j % 2:
            pairs[side, rows_of(turn_of(upper, j // 2))] = rows
        else:
            given[rows_of(turn_of(upper, j // 2))] = rows
        high, mid = split(rows)
        flats[j % 2] = flat.astype(BF16)
        parts[j % 2, :, :width] = high
        parts[j % 2, :, width:] = mid

    def send_sketch(j):
        i = j // 2
        for p in range(2 * i, min(2 * i + 2, raw)):
            (far_mine(p) if j % 2 else far_given(p)).start()
        if j % 2 == 0:
            give(turn_of(upper, i)).start()

    center(0)
    small_copies[0].wait()
    turned[...] = signs[...].astype(F32).T.astype(BF16)
    for j in range(2 * chunks):
        if j + 1 < 2 * chunks:
            center(j + 1)
        sketch(j)
        if j:
            wide[...] += dot(flats[(j - 1) % 2], parts[(j - 1) % 2])
        else:
            pl.semaphore_wait(barrier, size + 1)
        send_sketch(j)
    wide[...] += dot(flats[1], parts[1])
    turn = wide[:, width:]
    own = wide[:, :width] + turn + turn.T
    gram_part[...] = own.reshape(gram_part.shape)
    copies = scatter(gram_part, gram_recv, line, gram_send, gram_got)
    start(copies)

    def cross(i, carry):
        c = turn_of(upper, i)
        give(c).wait_recv()
        products[...] += cross_product(pairs[0, rows_of(c)], pairs[1, rows_of(c)])
        return carry

    lax.fori_loop(0, chunks, cross, 0)
    low_part[...] = products[...].reshape(low_part.shape)
    gram[coord] = summed(gram_part, gram_recv, line, copies)
    gathered = spread(gram, line, gram_send2, gram_got2)
    start(gathered)
    low_copies = scatter(low_part, low_recv, pair, low_send, low_got)
    start(low_copies)
    small_copies[1].wait()
    for l in range(2):
        outer[l] = dot_high(merge[l, 0], merge[l, 0], ((0,), (0,))) + dot_high(
            merge[l, 1], merge[l, 1], ((0,), (0,))
        )
    received(gathered)

    inverse_of(gram[...].reshape(width, width), x_ref)
    low_maps[upper, side] = dot_high(x_ref[...], merge[0, side], ((0,), (0,)))
    own_map = low_maps.at[upper, side]
    map_copies = [
        remote(own_map, own_map, map_send.at[i], map_got.at[i], device)
        for i, device in enumerate((partner, across))
    ]
    start(map_copies)
    low_gram[pair[0]] = summed(low_part, low_recv, pair, low_copies)
    low_gathered = spread(low_gram, pair, low_send2, low_got2)
    start(low_gathered)
    map_copies[0].wait_recv()
    for i in range(2):
        stack_map(stacks.at[0], i, low_maps[upper, i])

    def ship(which, p):
        rows = mixed.at[which, side, piece_of(which, p)]
        return remote(rows, rows, cross_send.at[p], cross_got.at[p], across)

    def share(which, c):
        far_side = lax.rem(which + upper, 2)
        rows = mixed.at[far_side, side, rows_of(c)]
        return remote(rows, rows, core_send.at[which, c], core_got.at[which, c], partner)

    def blend(i):
        c = turn_of(upper, i)
        mixed[upper, side, rows_of(c)] = mix_rows(
            pairs[0, rows_of(c)], pairs[1, rows_of(c)], stacks.at[0]
        )
        share(0, c).start()
        return c

    for i in list(range(raw // 2, chunks)) + list(range(raw // 2)):
        blend(i)
        for p in range(max(2 * i, raw), 2 * i + 2):
            ship(upper, p).start()
    map_copies[1].wait_recv()
    far_map = low_maps.at[1 - upper, side]
    map_copies.append(remote(far_map, far_map, map_send.at[2], map_got.at[2], partner))
    map_copies[2].start()
    map_copies[2].wait_recv()
    for i in range(2):
        stack_map(stacks.at[1], i, low_maps[1 - upper, i])

    products[...] = jnp.zeros_like(products)

    for p in range(2 * early):
        c = turn_of(1 - upper, p // 2)
        rows = piece_of(1 - upper, p)
        if p < raw:
            far_given(p).wait_recv()
            far_mine(p).wait_recv()
            mixed[1 - upper, side, rows] = mix_rows(far[0, p], far[1, p], stacks.at[1])
        else:
            ship(1 - upper, p).wait_recv()
        if p % 2:
            share(1, c).start()
        products[...] += cross_product(mixed[0, side, rows], mixed[1, side, rows])
    up_part[...] = products[...].reshape(up_part.shape)
    up_copies = scatter(up_part, up_recv, pair, up_send, up_got)
    start(up_copies)
    received(low_gathered)
    inner = dot_high(
        low_maps[upper, 0],
        dot_high(low_gram[...].reshape(width, width), low_maps[upper, 1], ((1,), (0,))),
        ((0,), (0,)),
    )
    inverse_of(outer[0] + inner + inner.T, x_ref)
    up_maps[upper] = dot_high(x_ref[...], merge[1, upper], ((0,), (0,)))
    up_gram[pair[0]] = summed(up_part, up_recv, pair, up_copies)
    up_gathered = spread(up_gram, pair, up_send2, up_got2)
    start(up_gathered)
    across_swap = remote(
        up_maps.at[upper], up_maps.at[upper], map_send.at[4], map_got.at[4], across
    )
    across_swap.start()

    projected[...] = jnp.zeros_like(projected)

    def project(h, i):
        c = turn_of(1 - upper, i)
        rows = jnp.concatenate(
            [mixed[0, h, rows_of(c)].astype(BF16), mixed[1, h, rows_of(c)].astype(BF16)], axis=1
        )
        place = 2 * lax.rem(i + early, chunks) + lax.rem(h + side + 1, 2)
        projected[...] += dot(held[place], rows)

    def project_given(i):
        c = turn_of(1 - upper, i)
        share(0, c).wait_recv()
        share(1, c).wait_recv()
        project(1 - side, i)

    def project_early(i, carry):
        project(side, i)
        project_given(i)
        return carry

    lax.fori_loop(0, early, project_early, 0)
    received(up_gathered)
    up_sides[upper] = up_gram[...].reshape(width, width)
    up_swap = remote(up_sides.at[upper], up_sides.at[upper], map_send.at[3], map_got.at[3], across)
    up_swap.start()
    for i in range(early, chunks):
        for p in range(2 * i, 2 * i + 2):
            ship(1 - upper, p).wait_recv()
        share(1, turn_of(1 - upper, i)).start()
        project(side, i)
    across_swap.wait_recv()
    for i in range(2):
        stack_map(stacks.at[0], i, up_maps[i])
    for i in range(early, chunks):
        project_given(i)

    block = score_part.shape[1]
    groups = n // 2
    group = coord // 2
    bit = lax.rem(coord, 2)

    def score_pair(g):
        rows = projected[pl.ds(pl.multiple_of(2 * g * block, 2 * block), 2 * block), :]
        both = mix_rows(rows[:, :width], rows[:, width:], stacks.at[0])
        score_part[2 * g] = both[:block]
        score_part[2 * g + 1] = both[block:]

    def hop(d):
        place = 2 * lax.rem(group + d, groups) + 1 - bit
        return remote(
            score_part.at[place], hop_recv.at[d], hop_send.at[d], hop_got.at[d],
            {"coord": coord + 1 - 2 * bit},
        )

    def relay(d):
        place = 2 * lax.rem(group + d, groups) + bit
        return remote(
            score_part.at[place], score_recv.at[d], score_send.at[d], score_got.at[d],
            {"coord": place},
        )

    for d in list(range(1, groups)) + [0]:
        score_pair(lax.rem(group + d, groups))
        hop(d).start()

    def between(t, tiles):
        for d in range(1, groups):
            if t == (tiles - 4) * d // (groups - 1):
                hop(d).wait_recv()
                place = 2 * lax.rem(group + d, groups) + bit
                score_part[place] = score_part[place] + hop_recv[d]
                relay(d).start()

    up_swap.wait_recv()
    inner = dot_high(
        up_maps[0],
        dot_high(up_sides[0] + up_sides[1], up_maps[1], ((1,), (0,))),
        ((0,), (0,)),
    )
    inverse_of(outer[1] + inner + inner.T, x_ref, between)
    for i in range(2):
        stack_map(stacks.at[1], i, dot_high(up_maps[i], x_ref[...], ((1,), (1,))) * grow)

    for c in range(chunks):
        for h in range(2):
            basis_ref[h, rows_of(c)] = mix_rows(
                mixed[0, h, rows_of(c)], mixed[1, h, rows_of(c)], stacks.at[1]
            )
    hop(0).wait_recv()
    total = score_part[coord] + hop_recv[0]
    for d in range(1, groups):
        relay(d).wait_recv()
        total = total + score_recv[d]
    scores_ref[...] = dot_high(total, x_ref[...], ((1,), (1,))) * scale

    sent(copies + gathered + low_copies + low_gathered + up_copies + up_gathered)
    sent(map_copies + [across_swap, up_swap])
    for d in range(groups):
        hop(d).wait_send()
        if d:
            relay(d).wait_send()
    for p in range(2 * chunks):
        if p < raw:
            far_given(p).wait_send()
            far_mine(p).wait_send()
        else:
            ship(upper, p).wait_send()
    for c in range(chunks):
        give(c).wait_send()
        share(0, c).wait_send()
        share(1, c).wait_send()


def store_kernel(basis_ref, scores_ref, basis_out, scores_out, sems):
    copies = [
        pltpu.make_async_copy(basis_ref.at[h], basis_out.at[h], sems.at[h]) for h in range(2)
    ]
    copies.append(pltpu.make_async_copy(scores_ref, scores_out, sems.at[2]))
    start(copies)
    for copy in copies:
        copy.wait()


def on_device(shapes, sketch_signs, merge_sketch):
    n = lax.axis_size("coord")
    _, subjects, coords = shapes.shape
    width = sketch_signs.shape[2]
    half = coords // 2
    tile = math.gcd(half // 2, 512)
    chunks = half // tile
    raw = max(1, 3 * chunks // 4)
    rows = subjects // n
    line = (n, width // n, width)
    pair = (2 * n, width // (2 * n), width)
    scale = 4.0 * math.sqrt(width / (coords * n))
    grow = math.sqrt(coords * n)
    vmem, dma = pltpu.VMEM, pltpu.SemaphoreType.DMA
    basis, scores = pl.pallas_call(
        functools.partial(whole_kernel, n, tile, scale, grow),
        out_shape=(
            jax.ShapeDtypeStruct((2, half, width), F32),
            jax.ShapeDtypeStruct((rows, width), F32),
        ),
        in_specs=[pl.BlockSpec(memory_space=pltpu.HBM)] * 3,
        out_specs=(pl.BlockSpec(memory_space=vmem), pl.BlockSpec(memory_space=vmem)),
        scratch_shapes=[
            vmem((2 * chunks, subjects, tile), BF16),
            vmem((subjects, width), jnp.int32),
            vmem(merge_sketch.shape, F32),
            vmem((width, subjects), BF16),
            vmem((half, width), F32),
            vmem((2, half, width), F32),
            vmem((2, raw, tile // 2, width), F32),
            vmem((2, 2, half, width), F32),
            vmem((2, 6 * width, width), BF16),
            vmem((2, 2, width, width), F32),
            vmem((2, width, width), F32),
            vmem((2, width, width), F32),
            vmem((width, width), F32),
            vmem((2, width, tile), BF16),
            vmem((2, tile, 2 * width), BF16),
            vmem((width, 2 * width), F32),
            vmem((width, width), F32),
            vmem((subjects, 2 * width), F32),
        ]
        + [vmem(line, F32)] * 3
        + [vmem(pair, F32)] * 6
        + [
            vmem((2, width, width), F32),
            vmem((n, rows, width), F32),
            vmem((n // 2, rows, width), F32),
            vmem((n // 2, rows, width), F32),
            dma((2 * chunks,)),
            dma((2,)),
        ]
        + [dma((chunks,))] * 2
        + [dma((2, raw))] * 2
        + [dma((2, chunks))] * 2
        + [dma((2 * chunks,))] * 2
        + [dma((n,))] * 4
        + [dma((n // 2,))] * 4
        + [dma((2 * n,))] * 8
        + [dma((5,))] * 2,
        compiler_params=pltpu.CompilerParams(
            collective_id=0, has_side_effects=True, vmem_limit_bytes=48 * 1024 * 1024
        ),
        name="shape_pca",
    )(
        shapes[0],
        pltpu.with_memory_space_constraint(sketch_signs[0], pltpu.HBM),
        pltpu.with_memory_space_constraint(merge_sketch, pltpu.HBM),
    )
    basis, scores = pl.pallas_call(
        store_kernel,
        out_shape=(
            jax.ShapeDtypeStruct(basis.shape, F32),
            jax.ShapeDtypeStruct(scores.shape, F32),
        ),
        in_specs=[pl.BlockSpec(memory_space=vmem)] * 2,
        out_specs=(pl.BlockSpec(memory_space=pltpu.HBM),) * 2,
        scratch_shapes=[dma((3,))],
        name="store",
    )(
        pltpu.with_memory_space_constraint(basis, pltpu.VMEM),
        pltpu.with_memory_space_constraint(scores, pltpu.VMEM),
    )
    return basis.reshape(1, coords, width), scores[None]


def solution(mesh):
    placed = (P("cohort", None, "coord"), P("cohort", None, None), P())
    return jax.shard_map(
        on_device,
        mesh=mesh,
        in_specs=placed,
        out_specs=(P("cohort", "coord", None), P("cohort", "coord", None)),
        check_vma=False,
    )
```
